128 devices in a mesh: seq: 32 (over x, z_lo, y), dp: 4 (over z_hi, core).
Axes of the slice: x: 4, y: 4, z: 4 (z_hi: 2, z_lo: 2; z = z_hi * 2 + z_lo), core: 2. Of those that a mesh axis runs over, the one named last changes fastest.
Arguments:
- probe_matrix: bfloat16 [4, 4096, 4096], P('dp', 'seq'), may hold values from -150 to 150
- softmax_lookup_matrix: bfloat16 [4, 4096, 4096], P('dp', 'seq'), may hold values from -6 to 6
- acceptance_gate: bfloat16 [4, 4096, 4096], P('dp', 'seq'), may hold values from -6 to 6
- recurrent_lookup_matrix: bfloat16 [4, 4096, 4096], P('dp', 'seq'), may hold values from -6 to 6
- recurrent_payload_matrix: bfloat16 [4, 4096, 4096], P('dp', 'seq'), may hold values from -6 to 6
- upstream_adjoint: bfloat16 [4, 4096, 4096], P('dp', 'seq'), may hold values from -6 to 6
- feature_fading_exponent: float32 [32, 128], replicated, may hold values from -20 to -3
- diagonal_reward_factor: float32 [32, 128], replicated, may hold values from -6 to 6
- spike_fading_exponent: float32 [4, 4096, 32], P('dp', 'seq'), may hold values from -1 to 0, as said below
Outputs:
- grad_queries: bfloat16 [4, 4096, 4096], P('dp', 'seq')
- grad_att_keys: bfloat16 [4, 4096, 4096], P('dp', 'seq')
- grad_receptance: bfloat16 [4, 4096, 4096], P('dp', 'seq')
- grad_mix_keys: bfloat16 [4, 4096, 4096], P('dp', 'seq')
- grad_mix_values: bfloat16 [4, 4096, 4096], P('dp', 'seq')
- fading_exponent_adjoint: float32 [32, 128], replicated
- diagonal_reward_adjoint: float32 [32, 128], replicated
The draws below stay inside these ranges and needn't reach their ends.
Inputs may be any that keep to these rules, and one draw needn't show every extreme that they name: `spike_fading_exponent`: zero at most positions.
All inputs are finite; a program needn't handle non-finite values.
Results may differ from the reference program's by a relative error of at most 0.0056.
Values may be sent and summed in bfloat16 or wider, within the bound.
No kernel may reach another device: no remote copies, remote signals or barrier semaphores. Data moves between devices by JAX's collectives and lax.ppermute only.
A program may use at most 192 MiB of HBM per device.

```python
import jax
import jax.numpy as jnp
from jax import lax

NUMBER_OF_HATS = 32
FEATURES_PER_HAT = 128
WINDOW = 512
TOK_DEV = 128
SEQLEN = 4096
BATCH_SEQUENCES = 4
WIDTH = 4096


def paired_rows(key):
    shape = (BATCH_SEQUENCES, SEQLEN, WIDTH)
    lookup_tile_matrix = jnp.clip(jax.random.normal(jax.random.fold_in(key, 101), shape, jnp.float32), -6.0, 6.0)
    query_rows = jnp.clip(jax.random.normal(jax.random.fold_in(key, 102), shape, jnp.float32), -6.0, 6.0)
    return (query_rows, lookup_tile_matrix)


def draw_probe_matrix(key, part):
    return paired_rows(key)[0].astype(jnp.bfloat16)


def draw_softmax_lookup_matrix(key, part):
    return paired_rows(key)[1].astype(jnp.bfloat16)


def draw_feature_fading_exponent(key, part):
    lowest = jnp.log(0.01 / SEQLEN)
    fastest = jnp.log(1.0 / 30.0)
    picked = jax.random.uniform(jax.random.fold_in(key, 201), (NUMBER_OF_HATS, FEATURES_PER_HAT), jnp.float32)
    return lowest + picked * (fastest - lowest)


def draw_spike_fading_exponent(key, part):
    shape = (BATCH_SEQUENCES, SEQLEN, NUMBER_OF_HATS)
    struck = jax.random.randint(jax.random.fold_in(key, 301), shape, 0, 384) == 0
    depth = jax.random.uniform(jax.random.fold_in(key, 302), shape, jnp.float32, -0.69, -0.22)
    return jnp.where(struck, depth, 0.0)


def steps_of(rng, dims, shards, low, high):
    def one(axis_at, parts):
        draws = jax.random.uniform(jax.random.fold_in(jax.random.fold_in(rng, 6), axis_at), (parts,), jnp.float32, low / len(shards), high / len(shards))
        return jnp.repeat(jnp.exp(draws), dims[axis_at] // parts).reshape((-1,) + (1,) * (len(dims) - axis_at - 1))

    gain = one(*shards[0])
    for cut in shards[1:]:
        gain = gain * one(*cut)
    return gain


def gaussian(key, extent, scale, most, cuts=(), held_as=jnp.bfloat16):
    loudness = steps_of(key, extent, cuts, -0.22, 0.18) if cuts else 1.0
    values = jax.random.normal(key, extent, jnp.float32) * scale * loudness
    return jnp.minimum(jnp.maximum(values, -most), most).astype(held_as)


def setup_inputs(seed: int = 0) -> dict:
    arg_keys = jax.random.split(jax.random.key(seed), 10)
    probe_matrix = draw_probe_matrix(jax.random.fold_in(arg_keys[9], 71), 0)
    softmax_lookup_matrix = draw_softmax_lookup_matrix(jax.random.fold_in(arg_keys[9], 71), 0)
    acceptance_gate = gaussian(arg_keys[2], (BATCH_SEQUENCES, SEQLEN, WIDTH), 1.0, 6.0, ((0, 4), (1, 32)))
    recurrent_lookup_matrix = gaussian(arg_keys[3], (BATCH_SEQUENCES, SEQLEN, WIDTH), 1.0, 6.0, ((0, 4), (1, 32)))
    recurrent_payload_matrix = gaussian(arg_keys[4], (BATCH_SEQUENCES, SEQLEN, WIDTH), 1.0, 6.0, ((0, 4), (1, 32)))
    upstream_adjoint = gaussian(arg_keys[5], (BATCH_SEQUENCES, SEQLEN, WIDTH), 1.0, 6.0, ((0, 4), (1, 32)))
    feature_fading_exponent = draw_feature_fading_exponent(jax.random.fold_in(arg_keys[9], 71), 0)
    diagonal_reward_factor = jnp.clip(jax.random.uniform(arg_keys[7], (NUMBER_OF_HATS, FEATURES_PER_HAT), jnp.float32, -6.0, 6.0), -6.0, 6.0)
    spike_fading_exponent = draw_spike_fading_exponent(jax.random.fold_in(arg_keys[9], 71), 0)
    return dict(probe_matrix=probe_matrix, softmax_lookup_matrix=softmax_lookup_matrix, acceptance_gate=acceptance_gate, recurrent_lookup_matrix=recurrent_lookup_matrix, recurrent_payload_matrix=recurrent_payload_matrix, upstream_adjoint=upstream_adjoint, feature_fading_exponent=feature_fading_exponent, diagonal_reward_factor=diagonal_reward_factor, spike_fading_exponent=spike_fading_exponent)


PRECISE = lax.Precision.HIGHEST
EPSILON = 1e-05

def rounded(payload_matrix):
    return payload_matrix + lax.stop_gradient(payload_matrix.astype(jnp.bfloat16).astype(jnp.float32) - payload_matrix)

def recurrence_tile(acceptance_matrix, lookup_tile_matrix, payload_matrix, fading_exponent, diagonal_reward_factor_arg, memory_arg):
    sequence_length = acceptance_matrix.shape[0]
    cumulative = jnp.cumsum(fading_exponent, axis=0)
    before = cumulative - fading_exponent
    attenuated_memory = acceptance_matrix * jnp.exp(before)
    key_scaled = lookup_tile_matrix * jnp.exp(-cumulative)
    scores = jnp.einsum('thi,shi->hts', attenuated_memory, key_scaled, precision=PRECISE)
    row_ids = lax.broadcasted_iota(jnp.int32, (sequence_length, sequence_length), 0)
    col_ids = lax.broadcasted_iota(jnp.int32, (sequence_length, sequence_length), 1)
    scores = jnp.where((col_ids < row_ids)[None], scores, 0.0)
    within_tile_summand = jnp.einsum('hts,shj->thj', scores, payload_matrix, precision=PRECISE)
    between_tiles_summand = jnp.einsum('thi,hij->thj', attenuated_memory, memory_arg, precision=PRECISE)
    diagonal_reward_summand = lax.optimization_barrier(jnp.sum(acceptance_matrix * diagonal_reward_factor_arg[None] * lookup_tile_matrix, axis=2, keepdims=True)) * payload_matrix
    total_decay = cumulative[-1]
    keys_end = lookup_tile_matrix * jnp.exp(total_decay[None] - cumulative)
    memory_result = jnp.exp(total_decay)[:, :, None] * memory_arg + jnp.einsum('thi,thj->hij', keys_end, payload_matrix, precision=PRECISE)
    return (between_tiles_summand + within_tile_summand + diagonal_reward_summand, memory_result, attenuated_memory)

def head_norm(module_result):
    average = lax.optimization_barrier(jnp.mean(module_result, axis=-1, keepdims=True))
    centered = module_result - average
    variance = lax.optimization_barrier(jnp.mean(centered * centered, axis=-1, keepdims=True))
    return centered * lax.rsqrt(variance + EPSILON)

def window_mask(sequence_length, reach, first_block):
    width = (reach + 1) * sequence_length
    row_ids = lax.broadcasted_iota(jnp.int32, (sequence_length, width), 0)
    col_ids = lax.broadcasted_iota(jnp.int32, (sequence_length, width), 1)
    return (col_ids > row_ids) & (col_ids <= row_ids + reach * sequence_length) & (col_ids // sequence_length >= first_block)

def attention_grads(query_rows, keys_all, values_all, cot_rows, first_block, reach):
    sequence_length = query_rows.shape[0]
    inv_root = query_rows.shape[2] ** (-0.5)
    scores = jnp.einsum('lhe,mhe->hlm', query_rows, keys_all, precision=PRECISE) * inv_root
    scores = jnp.where(window_mask(sequence_length, reach, first_block)[None], scores, -1e+30)
    highest = lax.optimization_barrier(jnp.max(scores, axis=2, keepdims=True))
    raised = jnp.exp(scores - highest)
    probabilities = raised / lax.optimization_barrier(jnp.sum(raised, axis=2, keepdims=True))
    weights = lax.optimization_barrier(probabilities.astype(jnp.bfloat16)).astype(jnp.float32)
    grad_weights = jnp.einsum('lhe,mhe->hlm', cot_rows, values_all, precision=PRECISE)
    delta_rows = lax.optimization_barrier(jnp.sum(probabilities * grad_weights, axis=2, keepdims=True))
    grad_scores = probabilities * (grad_weights - delta_rows) * inv_root
    probe_adjoint = jnp.einsum('hlm,mhe->lhe', grad_scores, keys_all, precision=PRECISE)
    grad_keys = jnp.einsum('hlm,lhe->mhe', grad_scores, query_rows, precision=PRECISE)
    grad_values = jnp.einsum('hlm,lhe->mhe', weights, cot_rows, precision=PRECISE)
    return (probe_adjoint, grad_keys, grad_values)

def reference(probe_matrix, softmax_lookup_matrix, acceptance_gate, recurrent_lookup_matrix, recurrent_payload_matrix, upstream_adjoint, feature_fading_exponent, diagonal_reward_factor, spike_fading_exponent):
    block_list = SEQLEN // TOK_DEV
    reach = WINDOW // TOK_DEV
    sequence_length = TOK_DEV

    def partition_tiles(array):
        return jnp.swapaxes(array.reshape((BATCH_SEQUENCES, block_list, sequence_length, NUMBER_OF_HATS, FEATURES_PER_HAT)), 0, 1).astype(jnp.float32)

    def flatten_tiles(array):
        return jnp.swapaxes(array, 0, 1).reshape((BATCH_SEQUENCES, SEQLEN, NUMBER_OF_HATS * FEATURES_PER_HAT))
    surge_block_list = jnp.swapaxes(spike_fading_exponent.reshape((BATCH_SEQUENCES, block_list, sequence_length, NUMBER_OF_HATS)), 0, 1)

    def recurrence_evaluate(acceptance_arg, recurrent_lookup_arg, recurrent_payload_arg, fading_exponent_arg, diagonal_reward_factor_arg):

        def mixing_step(running_memory, block_parts):
            acceptance_tile, lookup_tile, payload_tile, surge_block = block_parts
            fading_tile_entries = -jnp.exp(fading_exponent_arg)[None, None] + surge_block[..., None]
            module_result, successor_memory, discarded_result = jax.vmap(recurrence_tile, in_axes=(0, 0, 0, 0, None, 0))(acceptance_tile, lookup_tile, payload_tile, fading_tile_entries, diagonal_reward_factor_arg, running_memory)
            return (successor_memory, rounded(head_norm(module_result)))
        initial_empty_state = jnp.zeros((BATCH_SEQUENCES, NUMBER_OF_HATS, FEATURES_PER_HAT, FEATURES_PER_HAT), jnp.float32)
        ignored_state, mixed_output = lax.scan(jax.checkpoint(mixing_step), initial_empty_state, (acceptance_arg, recurrent_lookup_arg, recurrent_payload_arg, surge_block_list))
        return mixed_output
    blended_tile_entries, recurrence_adjoint_map = jax.vjp(recurrence_evaluate, partition_tiles(acceptance_gate), partition_tiles(recurrent_lookup_matrix), partition_tiles(recurrent_payload_matrix), feature_fading_exponent, diagonal_reward_factor)
    query_blocks = partition_tiles(probe_matrix)
    key_blocks = partition_tiles(softmax_lookup_matrix)
    cot_blocks = partition_tiles(upstream_adjoint)
    padding = jnp.zeros((reach,) + key_blocks.shape[1:], jnp.float32)
    key_pad = jnp.concatenate([padding, key_blocks], axis=0)
    mixed_pad = jnp.concatenate([padding, blended_tile_entries], axis=0)

    def window_rows(padded, block):
        taken = lax.dynamic_slice_in_dim(padded, block, reach + 1, 0)
        return jnp.moveaxis(taken, 0, 1).reshape((BATCH_SEQUENCES, (reach + 1) * sequence_length, NUMBER_OF_HATS, FEATURES_PER_HAT))

    def att_step(pending, block):
        pending_keys, pending_values = pending
        keys_all = window_rows(key_pad, block)
        values_all = window_rows(mixed_pad, block)
        query_blk = lax.dynamic_index_in_dim(query_blocks, block, 0, keepdims=False)
        cot_blk = lax.dynamic_index_in_dim(cot_blocks, block, 0, keepdims=False)
        first_block = (reach - block).astype(jnp.int32)
        probe_adjoint, grad_keys, grad_values = jax.vmap(lambda qrow, krow, vrow, crow: attention_grads(qrow, krow, vrow, crow, first_block, reach))(query_blk, keys_all, values_all, cot_blk)
        split = reach * sequence_length
        early_keys = jnp.moveaxis(grad_keys[:, :split].reshape((BATCH_SEQUENCES, reach, sequence_length, NUMBER_OF_HATS, FEATURES_PER_HAT)), 1, 0)
        early_values = jnp.moveaxis(grad_values[:, :split].reshape((BATCH_SEQUENCES, reach, sequence_length, NUMBER_OF_HATS, FEATURES_PER_HAT)), 1, 0)
        early_keys = lax.optimization_barrier(early_keys.astype(jnp.bfloat16)).astype(jnp.float32)
        early_values = lax.optimization_barrier(early_values.astype(jnp.bfloat16)).astype(jnp.float32)
        total_keys = grad_keys[:, split:] + pending_keys[0]
        total_values = cot_blk + grad_values[:, split:] + pending_values[0]
        zero_one = jnp.zeros_like(pending_keys[:1])
        next_keys = jnp.concatenate([pending_keys[1:], zero_one], axis=0) + early_keys[::-1]
        next_values = jnp.concatenate([pending_values[1:], zero_one], axis=0) + early_values[::-1]
        return ((next_keys, next_values), (probe_adjoint, total_keys, total_values))
    zero_pending = jnp.zeros((reach, BATCH_SEQUENCES, sequence_length, NUMBER_OF_HATS, FEATURES_PER_HAT), jnp.float32)
    unused_pending, (probe_adjoint, softmax_lookup_adjoint, blended_adjoint) = lax.scan(att_step, (zero_pending, zero_pending), jnp.arange(block_list, dtype=jnp.int32), reverse=True)
    acceptance_adjoint, recurrent_lookup_adjoint, recurrent_payload_adjoint, fading_exponent_adjoint, diagonal_reward_adjoint = recurrence_adjoint_map(blended_adjoint)
    normalizing_denominator = (BATCH_SEQUENCES * SEQLEN) ** (-0.5)
    return (flatten_tiles(probe_adjoint).astype(jnp.bfloat16), flatten_tiles(softmax_lookup_adjoint).astype(jnp.bfloat16), flatten_tiles(acceptance_adjoint).astype(jnp.bfloat16), flatten_tiles(recurrent_lookup_adjoint).astype(jnp.bfloat16), flatten_tiles(recurrent_payload_adjoint).astype(jnp.bfloat16), fading_exponent_adjoint * normalizing_denominator, diagonal_reward_adjoint * normalizing_denominator)
```

```python
import functools
import math

import jax
import jax.numpy as jnp
from jax import lax
from jax.experimental import pallas as pl
from jax.experimental.pallas import tpu as pltpu
from jax.sharding import PartitionSpec as P

F32 = jnp.float32
BF16 = jnp.bfloat16
EPSILON = 1e-05
NEG = -1e30
B = 128
REACH = 4
SPIKE_ROWS = 16
NN = (((1,), (0,)), ((), ()))
NT = (((1,), (1,)), ((), ()))
TN = (((0,), (0,)), ((), ()))


def dot(a, b, dims):
    return lax.dot_general(a, b, dims, preferred_element_type=F32)


def split(x):
    high = x.astype(BF16)
    return high, (x - high.astype(F32)).astype(BF16)


def dot_a(a, b, dims):
    return dot(a[0], b, dims) + dot(a[1], b, dims)


def dot_b(a, b, dims):
    return dot(a, b[0], dims) + dot(a, b[1], dims)


def dot3(a, b, dims):
    return dot(a[0], b[0], dims) + dot(a[0], b[1], dims) + dot(a[1], b[0], dims)


def iota(axis, shape=(B, B)):
    return lax.broadcasted_iota(jnp.int32, shape, axis)


def vmem():
    return pl.BlockSpec(memory_space=pltpu.VMEM)


def smem():
    return pl.BlockSpec(memory_space=pltpu.SMEM)


def params(mib=48):
    return pltpu.CompilerParams(vmem_limit_bytes=mib << 20)


def cost(flops, nbytes):
    return pl.CostEstimate(flops=int(flops), bytes_accessed=int(nbytes), transcendentals=0)


def three_parts(pair):
    row = iota(0, (SPIKE_ROWS, B))
    tile = jnp.zeros((SPIKE_ROWS, B), F32)
    for n, rest in enumerate(pair):
        for m in range(3):
            part = rest.astype(BF16).astype(F32)
            rest = rest - part
            tile = jnp.where(row == 3 * n + m, part, tile)
    return tile.astype(BF16)


def pack(arrays, spike, per=16):
    heads = arrays[0].shape[1] // B
    count = len(arrays)
    extra = 0 if spike is None else SPIKE_ROWS
    rows = count * B + extra

    def kernel(*refs):
        out = refs[-2] if extra else refs[-1]
        for j in range(per):
            for a in range(count):
                out[j, a * B : (a + 1) * B, :] = refs[a][:, j * B : (j + 1) * B]
        if extra:
            sums = refs[-1]
            step = pl.program_id(0)

            @pl.when(step == 0)
            def _():
                surge = refs[count][...]
                upto = jnp.where(iota(0) <= iota(1), 1.0, 0.0).astype(F32)
                below = jnp.where(iota(0) < iota(1), 1.0, 0.0).astype(F32)
                for n, mask in enumerate((upto, below)):
                    sums[n] = lax.dot_general(
                        surge, mask, NN, precision=lax.Precision.HIGHEST, preferred_element_type=F32
                    )

            for j in range(per):
                out[j, count * B :, :] = three_parts(
                    [sums[n, pl.ds(step * per + j, 1), :] for n in range(2)]
                )

    specs = [pl.BlockSpec((B, per * B), lambda i: (0, i)) for _ in arrays]
    operands = list(arrays)
    scratch = []
    if extra:
        specs.append(pl.BlockSpec(spike.shape, lambda i: (0, 0)))
        operands.append(spike)
        scratch = [pltpu.VMEM((2, heads, B), F32)]
    return pl.pallas_call(
        kernel,
        grid=(heads // per,),
        in_specs=specs,
        out_specs=pl.BlockSpec((per, rows, B), lambda i: (i, 0, 0)),
        out_shape=jax.ShapeDtypeStruct((heads, rows, B), BF16),
        scratch_shapes=scratch,
        cost_estimate=cost(0, 2 * heads * rows * B * 2),
        name="pack",
    )(*operands)


def unpack(packed, count, per=16):
    heads, rows, _ = packed.shape

    def kernel(x, *outs):
        for a in range(count):
            for j in range(per):
                outs[a][:, j * B : (j + 1) * B] = x[j, a * B : (a + 1) * B, :]

    return pl.pallas_call(
        kernel,
        grid=(heads // per,),
        in_specs=[pl.BlockSpec((per, rows, B), lambda i: (i, 0, 0))],
        out_specs=[pl.BlockSpec((B, per * B), lambda i: (0, i)) for _ in range(count)],
        out_shape=[jax.ShapeDtypeStruct((B, heads * B), BF16) for _ in range(count)],
        cost_estimate=cost(0, 2 * heads * count * B * B * 2),
        name="unpack",
    )(packed)


def decay_tables(rate, tables):
    position = iota(0).astype(F32)
    tables[0] = jnp.exp(-position * rate)
    tables[1] = jnp.exp((position + 1.0) * rate)
    tables[2] = jnp.exp(-(B - 1.0 - position) * rate)


def chunk_terms(x, n, tables, gain):
    base = 3 * B
    acceptance = x[n, 0:B, :].astype(F32)
    lookup = x[n, B : 2 * B, :].astype(F32)
    payload = x[n, 2 * B : 3 * B, :]
    surges = x[n, base : base + SPIKE_ROWS, :].astype(F32)
    upto = surges[0:1] + surges[1:2] + surges[2:3]
    below = surges[3:4] + surges[4:5] + surges[5:6]
    diagonal = iota(0) == iota(1)
    below_col = jnp.sum(jnp.where(diagonal, below, 0.0), axis=1, keepdims=True)
    upto_col = jnp.sum(jnp.where(diagonal, upto, 0.0), axis=1, keepdims=True)
    total = upto[:, B - 1 : B]
    lower = iota(1) < iota(0)
    fade = jnp.where(lower, jnp.exp(below_col - upto), 0.0)
    entered = jnp.exp(below_col)
    leaving = jnp.exp(total - upto_col)
    queries = acceptance * tables[0]
    keys = lookup * tables[1]
    keys_end = lookup * tables[2] * leaving
    bonus = jnp.sum(acceptance * gain * lookup, axis=1, keepdims=True)
    queries_s, keys_s = split(queries), split(keys)
    scores = dot3(queries_s, keys_s, NT) * fade + jnp.where(diagonal, bonus, 0.0)
    return dict(
        acceptance=acceptance,
        lookup=lookup,
        payload=payload,
        fade=fade,
        entered=entered,
        leaving=leaving,
        total=jnp.exp(total),
        queries=queries,
        queries_s=queries_s,
        keys_s=keys_s,
        keys_end=keys_end,
        keys_end_s=split(keys_end),
        scores=scores,
    )


def head_rows(index, fading, gain):
    return jnp.exp(fading[pl.ds(index, 1), :]), gain[pl.ds(index, 1), :]


def mix_forward(received, index, fading, gain, per=8):
    blocks, rows, _ = received.shape

    def kernel(index_ref, x, fading_ref, gain_ref, mixed, module, states, tables, memory):
        rate, gain_row = head_rows(index_ref[0], fading_ref, gain_ref)

        @pl.when(pl.program_id(0) == 0)
        def _():
            decay_tables(rate, tables)
            memory[...] = jnp.zeros_like(memory)

        whole = jnp.exp(-float(B) * rate)
        state = memory[...]
        for n in range(per):
            c = chunk_terms(x, n, tables, gain_row)
            states[n] = state
            out = dot_a(split(c["scores"]), c["payload"], NN) + c["entered"] * dot3(
                c["queries_s"], split(state), NT
            )
            state = state * (whole * c["total"]) + dot_b(c["payload"], c["keys_end_s"], TN)
            module[n] = out
            average = jnp.mean(out, axis=1, keepdims=True)
            centered = out - average
            variance = jnp.mean(centered * centered, axis=1, keepdims=True)
            mixed[n] = (centered * lax.rsqrt(variance + EPSILON)).astype(BF16)
        memory[...] = state

    block = lambda: pl.BlockSpec((per, B, B), lambda i: (i, 0, 0))
    whole_array = lambda a: pl.BlockSpec(a.shape, lambda i: (0, 0))
    return pl.pallas_call(
        kernel,
        grid=(blocks // per,),
        in_specs=[
            smem(),
            pl.BlockSpec((per, rows, B), lambda i: (i, 0, 0)),
            whole_array(fading),
            whole_array(gain),
        ],
        out_specs=[block(), block(), block()],
        out_shape=[
            jax.ShapeDtypeStruct((blocks, B, B), BF16),
            jax.ShapeDtypeStruct((blocks, B, B), F32),
            jax.ShapeDtypeStruct((blocks, B, B), F32),
        ],
        scratch_shapes=[pltpu.VMEM((3, B, B), F32), pltpu.VMEM((B, B), F32)],
        compiler_params=params(),
        cost_estimate=cost(2e10, 8 << 20),
        name="mix_forward",
    )(index, received, fading, gain)


def mix_backward(received, gradient, module, states, index, fading, gain, per=4):
    blocks, rows, _ = received.shape
    steps = blocks // per

    def kernel(
        index_ref, x, g_ref, module_ref, states_ref, fading_ref, gain_ref, out, tables, memory, sums
    ):
        rate, gain_row = head_rows(index_ref[0], fading_ref, gain_ref)

        @pl.when(pl.program_id(0) == 0)
        def _():
            decay_tables(rate, tables)
            memory[...] = jnp.zeros_like(memory)
            sums[...] = jnp.zeros_like(sums)

        whole = jnp.exp(-float(B) * rate)
        position = iota(0).astype(F32)
        distance = jnp.maximum(iota(0) - iota(1) - 1, 0).astype(F32)
        d_state = memory[...]
        d_rate = jnp.zeros((1, B), F32)
        d_gain = jnp.zeros((1, B), F32)
        first = (steps - 1 - pl.program_id(0)) * per
        for n in reversed(range(per)):
            c = chunk_terms(x, n, tables, gain_row)
            value = module_ref[n]
            centered = value - jnp.mean(value, axis=1, keepdims=True)
            variance = jnp.mean(centered * centered, axis=1, keepdims=True)
            scale = lax.rsqrt(variance + EPSILON)
            normed = centered * scale
            g = g_ref[n]
            grad = scale * (
                g
                - jnp.mean(g, axis=1, keepdims=True)
                - normed * jnp.mean(g * normed, axis=1, keepdims=True)
            )
            grad_s = split(grad)
            state = states_ref[n]
            state_s, d_state_s = split(state), split(d_state)
            payload = c["payload"]
            paired = dot_a(grad_s, payload, NT) * c["fade"]
            paired_s = split(paired)
            own = jnp.sum(grad * payload.astype(F32), axis=1, keepdims=True)
            inter = c["entered"] * dot3(grad_s, state_s, NN)
            d_queries = dot3(paired_s, c["keys_s"], NN) + inter
            d_keys = dot3(paired_s, c["queries_s"], TN)
            d_end = dot_b(payload, d_state_s, NN)
            d_payload = dot3(split(c["scores"]), grad_s, TN) + dot3(c["keys_end_s"], d_state_s, NT)
            out[first + n, 0:B, :] = (
                d_queries * tables[0] + own * gain_row * c["lookup"]
            ).astype(BF16)
            out[first + n, B : 2 * B, :] = (
                d_keys * tables[1]
                + d_end * (tables[2] * c["leaving"])
                + own * gain_row * c["acceptance"]
            ).astype(BF16)
            out[first + n, 2 * B : 3 * B, :] = d_payload.astype(BF16)
            d_gain += jnp.sum(own * c["acceptance"] * c["lookup"], axis=0, keepdims=True)
            spread = dot(
                (paired * distance).astype(BF16), c["keys_s"][0], NN
            )
            carried = whole * c["total"]
            d_rate += jnp.sum(
                c["queries"] * (spread + position * inter)
                + (B - 1.0 - position) * c["keys_end"] * d_end
                + (float(B) * carried) * state * d_state,
                axis=0,
                keepdims=True,
            )
            d_state = d_state * carried + dot3(
                split(grad * c["entered"]), c["queries_s"], TN
            )
        memory[...] = d_state
        sums[0:1, :] += -rate * d_rate
        sums[1:2, :] += d_gain

        @pl.when(pl.program_id(0) == steps - 1)
        def _():
            tile = three_parts([sums[0:1, :], sums[1:2, :]])
            for b in range(blocks):
                out[b, 3 * B :, :] = tile

    back = lambda i: (steps - 1 - i, 0, 0)
    block = lambda: pl.BlockSpec((per, B, B), back)
    whole_array = lambda a: pl.BlockSpec(a.shape, lambda i: (0, 0))
    return pl.pallas_call(
        kernel,
        grid=(steps,),
        in_specs=[
            smem(),
            pl.BlockSpec((per, rows, B), back),
            block(),
            block(),
            block(),
            whole_array(fading),
            whole_array(gain),
        ],
        out_specs=vmem(),
        out_shape=jax.ShapeDtypeStruct((blocks, rows, B), BF16),
        scratch_shapes=[
            pltpu.VMEM((3, B, B), F32),
            pltpu.VMEM((B, B), F32),
            pltpu.VMEM((8, B), F32),
        ],
        compiler_params=params(),
        cost_estimate=cost(2e10, 12 << 20),
        name="mix_backward",
    )(index, received, gradient, module, states, fading, gain)


def attention_grads(received, mixed):
    blocks = received.shape[0]
    pad = REACH * B
    length = blocks * B
    two = 2 * B
    span = pad + two
    inv_root = B ** (-0.5)
    to_log2 = inv_root * math.log2(math.e)

    def kernel(x, m_ref, out, gm, kpad, mpad, dk, dm, s_t, dp_t, w_t, ds_t):
        kpad[0:pad, :] = jnp.zeros((pad, B), BF16)
        mpad[0:pad, :] = jnp.zeros((pad, B), BF16)
        dk[...] = jnp.zeros_like(dk)
        dm[...] = jnp.zeros_like(dm)
        for ref in (w_t, ds_t):
            ref[pad + B :, 0:B] = jnp.zeros((B, B), BF16)
            ref[0:B, B:] = jnp.zeros((B, B), BF16)

        def fill(b, _):
            at = pl.ds(pl.multiple_of(pad + b * B, B), B)
            kpad[at, :] = x[b, B : 2 * B, :]
            mpad[at, :] = m_ref[b]
            return 0

        lax.fori_loop(0, blocks, fill, 0)
        early = iota(0) > iota(1)
        causal = iota(0) <= iota(1)

        def step(i, _, first=None):
            rows = pl.ds(pl.multiple_of(i * two, two), span)
            queries = jnp.concatenate([x[2 * i, 0:B, :], x[2 * i + 1, 0:B, :]], axis=0)
            cots = jnp.concatenate(
                [x[2 * i, 2 * B : 3 * B, :], x[2 * i + 1, 2 * B : 3 * B, :]], axis=0
            )
            keys = kpad[rows, :]
            s_t[...] = dot(keys, queries, NT)
            dp_t[...] = dot(mpad[rows, :], cots, NT)
            for sub in range(2):
                lanes = slice(sub * B, (sub + 1) * B)
                pick = [slice((sub + j) * B, (sub + j + 1) * B) for j in range(REACH + 1)]
                live = [
                    j
                    for j in range(REACH + 1)
                    if first is None or 2 * first + sub - REACH + j >= 0
                ]
                scores = {}
                for j in live:
                    score = s_t[pick[j], lanes]
                    if j == 0:
                        score = jnp.where(early, score, NEG)
                    if j == REACH:
                        score = jnp.where(causal, score, NEG)
                    scores[j] = score
                highest = functools.reduce(
                    jnp.maximum, [jnp.max(scores[j], axis=0, keepdims=True) for j in live]
                )
                raised = {j: jnp.exp2((scores[j] - highest) * to_log2) for j in live}
                total = sum(jnp.sum(raised[j], axis=0, keepdims=True) for j in live)
                inner = sum(
                    jnp.sum(raised[j] * dp_t[pick[j], lanes], axis=0, keepdims=True) for j in live
                )
                share = 1.0 / total
                delta = inner * share
                for j in range(REACH + 1):
                    if j in live:
                        probability = raised[j] * share
                        w_t[pick[j], lanes] = probability.astype(BF16)
                        ds_t[pick[j], lanes] = (
                            probability * ((dp_t[pick[j], lanes] - delta) * inv_root)
                        ).astype(BF16)
                    else:
                        w_t[pick[j], lanes] = jnp.zeros((B, B), BF16)
                        ds_t[pick[j], lanes] = jnp.zeros((B, B), BF16)
            dk[rows, :] += dot(ds_t[...], queries, NN)
            dm[rows, :] += dot(w_t[...], cots, NN)
            dq = dot(ds_t[...], keys, TN).astype(BF16)
            out[2 * i, 0:B, :] = dq[0:B]
            out[2 * i + 1, 0:B, :] = dq[B:]
            return 0

        for i in range(REACH // 2):
            step(i, 0, first=i)
        lax.fori_loop(REACH // 2, blocks // 2, step, 0)

        def flush(b, _):
            at = pl.ds(pl.multiple_of(pad + b * B, B), B)
            out[b, B : 2 * B, :] = dk[at, :].astype(BF16)
            gm[b] = dm[at, :] + x[b, 2 * B : 3 * B, :].astype(F32)
            return 0

        lax.fori_loop(0, blocks, flush, 0)

    return pl.pallas_call(
        kernel,
        in_specs=[vmem(), vmem()],
        out_specs=[vmem(), vmem()],
        out_shape=[
            jax.ShapeDtypeStruct((blocks, 2 * B, B), BF16),
            jax.ShapeDtypeStruct((blocks, B, B), F32),
        ],
        scratch_shapes=[
            pltpu.VMEM((pad + length, B), BF16),
            pltpu.VMEM((pad + length, B), BF16),
            pltpu.VMEM((pad + length, B), F32),
            pltpu.VMEM((pad + length, B), F32),
            pltpu.VMEM((span, two), F32),
            pltpu.VMEM((span, two), F32),
            pltpu.VMEM((span, two), BF16),
            pltpu.VMEM((span, two), BF16),
        ],
        compiler_params=params(),
        cost_estimate=cost(2e10, 8 << 20),
        name="attention_grads",
    )(received, mixed)


def exchange(blocks):
    return lax.all_to_all(blocks, "seq", 0, 0, tiled=True)


def local(
    probe_matrix,
    softmax_lookup_matrix,
    acceptance_gate,
    recurrent_lookup_matrix,
    recurrent_payload_matrix,
    upstream_adjoint,
    feature_fading_exponent,
    diagonal_reward_factor,
    spike_fading_exponent,
):
    positions = probe_matrix.shape[1] * lax.axis_size("seq") * lax.axis_size("dp")
    here = lax.axis_index("seq")
    index = here.astype(jnp.int32).reshape(1)
    mix_in = exchange(
        pack(
            (acceptance_gate[0], recurrent_lookup_matrix[0], recurrent_payload_matrix[0]),
            spike_fading_exponent[0].T,
        )
    )
    att_in = exchange(
        pack((probe_matrix[0], softmax_lookup_matrix[0], upstream_adjoint[0]), None)
    )
    mixed, module, states = mix_forward(
        mix_in, index, feature_fading_exponent, diagonal_reward_factor
    )
    att_out, gradient = attention_grads(att_in, mixed)
    att_back = exchange(att_out)
    mix_out = mix_backward(
        mix_in, gradient, module, states, index, feature_fading_exponent, diagonal_reward_factor
    )
    mix_out, att_back = lax.optimization_barrier((mix_out, att_back))
    mix_back = exchange(mix_out)
    parts = mix_back[:, 3 * B : 3 * B + 6, :].astype(F32)
    sums = jnp.stack([parts[:, 0] + parts[:, 1] + parts[:, 2], parts[:, 3] + parts[:, 4] + parts[:, 5]])
    group = lax.axis_size("dp")
    around = [
        lax.ppermute(sums, "dp", [(i, (i + k) % group) for i in range(group)])
        for k in range(1, group)
    ]
    adjoints = ((sums + around[1]) + (around[0] + around[2])) * positions ** (-0.5)
    dq, dk = unpack(att_back, 2)
    dr, dmk, dmv = unpack(mix_back, 3)
    return (dq[None], dk[None], dr[None], dmk[None], dmv[None], adjoints[0], adjoints[1])


def solution(mesh):
    rows = P("dp", "seq", None)
    return jax.shard_map(
        local,
        mesh=mesh,
        in_specs=(rows,) * 6 + (P(), P(), rows),
        out_specs=(rows,) * 5 + (P(), P()),
        check_vma=False,
    )
```

```python
import functools
import math

import jax
import jax.numpy as jnp
from jax import lax
from jax.experimental import pallas as pl
from jax.experimental.pallas import tpu as pltpu
from jax.sharding import PartitionSpec as P

F32 = jnp.float32
BF16 = jnp.bfloat16
EPSILON = 1e-05
NEG = -1e30
LOG2E = math.log2(math.e)
B = 128
REACH = 4
SPIKE_ROWS = 16
QUERIES = 3 * B
KEYS = 4 * B
SPIKES = 5 * B
SUMS = 3 * B
PAD = REACH * B
TWO = 2 * B
SPAN = PAD + TWO
INV_ROOT = B ** (-0.5)
NN = (((1,), (0,)), ((), ()))
NT = (((1,), (1,)), ((), ()))
TN = (((0,), (0,)), ((), ()))


def dot(a, b, dims):
    return lax.dot_general(a, b, dims, preferred_element_type=F32)


def split(x):
    high = x.astype(BF16)
    return high, (x - high.astype(F32)).astype(BF16)


def dot_a(a, b, dims):
    return dot(a[0], b, dims) + dot(a[1], b, dims)


def dot_b(a, b, dims):
    return dot(a, b[0], dims) + dot(a, b[1], dims)


def dot3(a, b, dims):
    return dot(a[0], b[0], dims) + dot(a[0], b[1], dims) + dot(a[1], b[0], dims)


def iota(axis, shape=(B, B)):
    return lax.broadcasted_iota(jnp.int32, shape, axis)


def vmem():
    return pl.BlockSpec(memory_space=pltpu.VMEM)


def smem():
    return pl.BlockSpec(memory_space=pltpu.SMEM)


def params(mib=58):
    return pltpu.CompilerParams(vmem_limit_bytes=mib << 20)


def cost(flops, nbytes):
    return pl.CostEstimate(flops=int(flops), bytes_accessed=int(nbytes), transcendentals=0)


def three_parts(pair):
    row = iota(0, (SPIKE_ROWS, B))
    tile = jnp.zeros((SPIKE_ROWS, B), F32)
    for n, rest in enumerate(pair):
        for m in range(3):
            part = rest.astype(BF16).astype(F32)
            rest = rest - part
            tile = jnp.where(row == 3 * n + m, part, tile)
    return tile.astype(BF16)


def pack(arrays, cots, spike, per=8):
    heads = cots.shape[1] // B
    count = len(arrays)
    steps = heads // per
    rows = SPIKES + SPIKE_ROWS

    def kernel(*refs):
        sources, surge_ref = refs[: count + 1], refs[count + 1]
        first, second, first_buf, second_buf, sums, first_sem, second_sem = refs[count + 2 :]
        step = pl.program_id(0)

        def leaving(h):
            return pltpu.make_async_copy(first_buf.at[h], first.at[h], first_sem.at[h])

        def leaving_cots(g):
            at = pl.ds(g * per, per)
            return pltpu.make_async_copy(second_buf.at[at], second.at[at], second_sem.at[g])

        @pl.when(step == 0)
        def _():
            surge = surge_ref[...]
            upto = jnp.where(iota(0) <= iota(1), 1.0, 0.0).astype(F32)
            below = jnp.where(iota(0) < iota(1), 1.0, 0.0).astype(F32)
            for n, mask in enumerate((upto, below)):
                sums[n] = lax.dot_general(
                    surge, mask, NN, precision=lax.Precision.HIGHEST, preferred_element_type=F32
                )

        for j in range(per):
            h = step * per + j
            columns = slice(j * B, (j + 1) * B)
            for a in range(count):
                first_buf[h, a * B : (a + 1) * B, :] = sources[a][:, columns]
            first_buf[h, SPIKES:, :] = three_parts([sums[n, pl.ds(h, 1), :] for n in range(2)])
            leaving(h).start()
            second_buf[h] = sources[count][:, columns]
        leaving_cots(step).start()

        @pl.when(step == steps - 1)
        def _():
            for h in range(heads):
                leaving(h).wait()
            for g in range(steps):
                leaving_cots(g).wait()

    return pl.pallas_call(
        kernel,
        grid=(steps,),
        in_specs=[pl.BlockSpec((B, per * B), lambda i: (0, i)) for _ in range(count + 1)]
        + [pl.BlockSpec(spike.shape, lambda i: (0, 0))],
        out_specs=[pl.BlockSpec(memory_space=pl.ANY)] * 2,
        out_shape=[
            jax.ShapeDtypeStruct((heads, rows, B), BF16),
            jax.ShapeDtypeStruct((heads, B, B), BF16),
        ],
        scratch_shapes=[
            pltpu.VMEM((heads, rows, B), BF16),
            pltpu.VMEM((heads, B, B), BF16),
            pltpu.VMEM((2, heads, B), F32),
            pltpu.SemaphoreType.DMA((heads,)),
            pltpu.SemaphoreType.DMA((steps,)),
        ],
        compiler_params=params(),
        cost_estimate=cost(0, 2 * heads * (rows + B) * B * 2),
        name="pack",
    )(*arrays, cots, spike)


def unpack(packed, count, per=16):
    heads, rows, _ = packed.shape

    def kernel(x, *outs):
        for a in range(count):
            for j in range(per):
                outs[a][:, j * B : (j + 1) * B] = x[j, a * B : (a + 1) * B, :]

    return pl.pallas_call(
        kernel,
        grid=(heads // per,),
        in_specs=[pl.BlockSpec((per, rows, B), lambda i: (i, 0, 0))],
        out_specs=[pl.BlockSpec((B, per * B), lambda i: (0, i)) for _ in range(count)],
        out_shape=[jax.ShapeDtypeStruct((B, heads * B), BF16) for _ in range(count)],
        compiler_params=params(12),
        cost_estimate=cost(0, 2 * heads * count * B * B * 2),
        name="unpack",
    )(packed)


def decay_tables(rate, tables):
    position = iota(0).astype(F32)
    tables[0] = jnp.exp(-position * rate)
    tables[1] = jnp.exp((position + 1.0) * rate)
    tables[2] = jnp.exp(-(B - 1.0 - position) * rate)


def chunk_terms(x, surges, tables, gain, n, exact=True):
    acceptance = x[n, 0:B, :].astype(F32)
    lookup = x[n, B : 2 * B, :].astype(F32)
    payload = x[n, 2 * B : 3 * B, :]
    upto = surges[0:1] + surges[1:2] + surges[2:3]
    below = surges[3:4] + surges[4:5] + surges[5:6]
    diagonal = iota(0) == iota(1)
    below_col = jnp.sum(jnp.where(diagonal, below, 0.0), axis=1, keepdims=True)
    upto_col = jnp.sum(jnp.where(diagonal, upto, 0.0), axis=1, keepdims=True)
    total = upto[:, B - 1 : B]
    lower = iota(1) < iota(0)
    fade = jnp.where(lower, jnp.exp(below_col - upto), 0.0)
    entered = jnp.exp(below_col)
    leaving = jnp.exp(total - upto_col)
    queries = acceptance * tables[0]
    keys = lookup * tables[1]
    keys_end = lookup * tables[2] * leaving
    bonus = jnp.sum(acceptance * gain * lookup, axis=1, keepdims=True)
    if exact:
        queries_s, keys_s = split(queries), split(keys)
        keys_end_s = split(keys_end)
        scores = dot3(queries_s, keys_s, NT)
    else:
        queries_s, keys_s = queries.astype(BF16), keys.astype(BF16)
        keys_end_s = keys_end.astype(BF16)
        scores = dot(queries_s, keys_s, NT)
    scores = scores * fade + jnp.where(diagonal, bonus, 0.0)
    return dict(
        acceptance=acceptance,
        lookup=lookup,
        payload=payload,
        fade=fade,
        entered=entered,
        leaving=leaving,
        total=jnp.exp(total),
        queries=queries,
        queries_s=queries_s,
        keys_s=keys_s,
        keys_end=keys_end,
        keys_end_s=keys_end_s,
        scores=scores,
    )


def head_rows(index, fading, gain):
    return jnp.exp(fading[pl.ds(index, 1), :]), gain[pl.ds(index, 1), :]


def attention_weights(keys, queries, step, weights, n):
    scores_all = dot(keys, queries, NT)
    early = iota(0) > iota(1)
    causal = iota(0) <= iota(1)
    for sub in range(2):
        lanes = slice(sub * B, (sub + 1) * B)
        scores = []
        for j in range(REACH + 1):
            score = scores_all[(sub + j) * B : (sub + j + 1) * B, lanes]
            if j == REACH:
                keep = causal
            else:
                keep = 2 * step + sub + j >= REACH
                if j == 0:
                    keep = early & keep
            scores.append(jnp.where(keep, score, NEG))
        highest = jnp.max(functools.reduce(jnp.maximum, scores), axis=0, keepdims=True)
        raised = [jnp.exp2((score - highest) * (INV_ROOT * LOG2E)) for score in scores]
        share = 1.0 / jnp.sum(sum(raised), axis=0, keepdims=True)
        for j in range(REACH + 1):
            weights[n, (sub + j) * B : (sub + j + 1) * B, lanes] = (raised[j] * share).astype(BF16)
    weights[n, PAD + B :, 0:B] = jnp.zeros((B, B), BF16)
    weights[n, 0:B, B:] = jnp.zeros((B, B), BF16)


def forward(received, index, fading, gain, per=8):
    blocks, rows, _ = received.shape

    def kernel(
        index_ref, x, fading_ref, gain_ref, mixed, module, states, weights, turned,
        tables, memory, kring,
    ):
        rate, gain_row = head_rows(index_ref[0], fading_ref, gain_ref)
        grid_step = pl.program_id(0)

        @pl.when(grid_step == 0)
        def _():
            decay_tables(rate, tables)
            memory[...] = jnp.zeros_like(memory)
            kring[0:PAD, :] = jnp.zeros((PAD, B), BF16)

        whole = jnp.exp(-float(B) * rate)
        state = memory[...]
        for n in range(per):
            keys = x[n, KEYS : KEYS + B, :]
            kring[pl.ds(pl.multiple_of(PAD + (grid_step * per + n) * B, B), B), :] = keys
            turned[n] = keys.T
            c = chunk_terms(
                x, x[n, SPIKES : SPIKES + SPIKE_ROWS, :].astype(F32), tables, gain_row, n
            )
            states[n] = state
            out = dot_a(split(c["scores"]), c["payload"], NN) + c["entered"] * dot3(
                c["queries_s"], split(state), NT
            )
            state = state * (whole * c["total"]) + dot_b(c["payload"], c["keys_end_s"], TN)
            module[n] = out
            average = jnp.mean(out, axis=1, keepdims=True)
            centered = out - average
            variance = jnp.mean(centered * centered, axis=1, keepdims=True)
            mixed[n] = (centered * lax.rsqrt(variance + EPSILON)).astype(BF16)
            if n % 2:
                step = grid_step * (per // 2) + n // 2
                attention_weights(
                    kring[pl.ds(pl.multiple_of(step * TWO, TWO), SPAN), :],
                    jnp.concatenate(
                        [x[n - 1, QUERIES : QUERIES + B, :], x[n, QUERIES : QUERIES + B, :]], axis=0
                    ),
                    step,
                    weights,
                    n // 2,
                )
        memory[...] = state

    block = lambda: pl.BlockSpec((per, B, B), lambda i: (i, 0, 0))
    whole_array = lambda a: pl.BlockSpec(a.shape, lambda i: (0, 0))
    return pl.pallas_call(
        kernel,
        grid=(blocks // per,),
        in_specs=[
            smem(),
            pl.BlockSpec((per, rows, B), lambda i: (i, 0, 0)),
            whole_array(fading),
            whole_array(gain),
        ],
        out_specs=[
            block(),
            block(),
            block(),
            pl.BlockSpec((per // 2, SPAN, TWO), lambda i: (i, 0, 0)),
            block(),
        ],
        out_shape=[
            jax.ShapeDtypeStruct((blocks, B, B), BF16),
            jax.ShapeDtypeStruct((blocks, B, B), F32),
            jax.ShapeDtypeStruct((blocks, B, B), F32),
            jax.ShapeDtypeStruct((blocks // 2, SPAN, TWO), BF16),
            jax.ShapeDtypeStruct((blocks, B, B), BF16),
        ],
        scratch_shapes=[
            pltpu.VMEM((3, B, B), F32),
            pltpu.VMEM((B, B), F32),
            pltpu.VMEM((PAD + blocks * B, B), BF16),
        ],
        compiler_params=params(),
        cost_estimate=cost(2e10, 18 << 20),
        name="forward",
    )(index, received, fading, gain)


def pair_of(ref, at):
    return jnp.concatenate([ref[2 * at], ref[2 * at + 1]], axis=0)


def mix_backward(received, weights, cots, module, states, index, fading, gain, per=4):
    blocks = received.shape[0]
    rows = SUMS + SPIKE_ROWS
    steps = blocks // per

    def kernel(
        index_ref, x, surge_ref, w0_ref, w1_ref, w2_ref, cot_ref, module_ref, states_ref, fading_ref, gain_ref,
        out, tables, memory, sums,
    ):
        rate, gain_row = head_rows(index_ref[0], fading_ref, gain_ref)

        @pl.when(pl.program_id(0) == 0)
        def _():
            decay_tables(rate, tables)
            memory[...] = jnp.zeros_like(memory)
            sums[...] = jnp.zeros_like(sums)

        whole = jnp.exp(-float(B) * rate)
        position = iota(0).astype(F32)
        distance = jnp.maximum(iota(0) - iota(1) - 1, 0).astype(F32)
        d_state = memory[...]
        d_rate = jnp.zeros((1, B), F32)
        d_gain = jnp.zeros((1, B), F32)
        first = (steps - 1 - pl.program_id(0)) * per
        for n in reversed(range(per)):
            if n % 2:
                pair_at = first // 2 + n // 2
                g_pair = pair_of(cot_ref, pair_at).astype(F32)
                for later in range(3):
                    at = jnp.minimum(pair_at + later, blocks // 2 - 1)
                    seen = pair_of(cot_ref, at)
                    if later:
                        seen = jnp.where(pair_at + later < blocks // 2, seen, jnp.zeros_like(seen))
                    seen_by = (w2_ref, w1_ref, w0_ref)[later]
                    g_pair = g_pair + dot(seen_by[at], seen, NN)
            g = g_pair[B:] if n % 2 else g_pair[0:B]
            c = chunk_terms(x, surge_ref[n].astype(F32), tables, gain_row, n, False)
            value = module_ref[n]
            centered = value - jnp.mean(value, axis=1, keepdims=True)
            variance = jnp.mean(centered * centered, axis=1, keepdims=True)
            scale = lax.rsqrt(variance + EPSILON)
            normed = centered * scale
            grad = scale * (
                g
                - jnp.mean(g, axis=1, keepdims=True)
                - normed * jnp.mean(g * normed, axis=1, keepdims=True)
            )
            grad_s = grad.astype(BF16)
            state = states_ref[n]
            d_state_s = d_state.astype(BF16)
            payload = c["payload"]
            paired = dot(grad_s, payload, NT) * c["fade"]
            paired_s = paired.astype(BF16)
            own = jnp.sum(grad * payload.astype(F32), axis=1, keepdims=True)
            inter = c["entered"] * dot(grad_s, state.astype(BF16), NN)
            d_queries = dot(paired_s, c["keys_s"], NN) + inter
            d_keys = dot(paired_s, c["queries_s"], TN)
            d_end = dot(payload, d_state_s, NN)
            d_payload = dot(c["scores"].astype(BF16), grad_s, TN) + dot(
                c["keys_end_s"], d_state_s, NT
            )
            out[first + n, 0:B, :] = (
                d_queries * tables[0] + own * gain_row * c["lookup"]
            ).astype(BF16)
            out[first + n, B : 2 * B, :] = (
                d_keys * tables[1]
                + d_end * (tables[2] * c["leaving"])
                + own * gain_row * c["acceptance"]
            ).astype(BF16)
            out[first + n, 2 * B : 3 * B, :] = d_payload.astype(BF16)
            d_gain += jnp.sum(own * c["acceptance"] * c["lookup"], axis=0, keepdims=True)
            spread = dot((paired * distance).astype(BF16), c["keys_s"], NN)
            carried = whole * c["total"]
            d_rate += jnp.sum(
                c["queries"] * (spread + position * inter)
                + (B - 1.0 - position) * c["keys_end"] * d_end
                + (float(B) * carried) * state * d_state,
                axis=0,
                keepdims=True,
            )
            d_state = d_state * carried + dot(
                (grad * c["entered"]).astype(BF16), c["queries_s"], TN
            )
        memory[...] = d_state
        sums[0:1, :] += -rate * d_rate
        sums[1:2, :] += d_gain

        @pl.when(pl.program_id(0) == steps - 1)
        def _():
            tile = three_parts([sums[0:1, :], sums[1:2, :]])
            for b in range(blocks):
                out[b, SUMS:, :] = tile

    back = lambda i: (steps - 1 - i, 0, 0)
    block = lambda: pl.BlockSpec((per, B, B), back)
    whole_array = lambda a: pl.BlockSpec(a.shape, lambda i: (0, 0))
    return pl.pallas_call(
        kernel,
        grid=(steps,),
        in_specs=[
            smem(),
            pl.BlockSpec((per, SUMS, B), back),
            pl.BlockSpec((per, SPIKE_ROWS, B), lambda i: (steps - 1 - i, SPIKES // SPIKE_ROWS, 0)),
            *(
                pl.BlockSpec((blocks // 2, TWO, TWO), functools.partial(lambda j, i: (0, j, 0), j))
                for j in range(3)
            ),
            pl.BlockSpec(cots.shape, lambda i: (0, 0, 0)),
            block(),
            block(),
            whole_array(fading),
            whole_array(gain),
        ],
        out_specs=vmem(),
        out_shape=jax.ShapeDtypeStruct((blocks, rows, B), BF16),
        scratch_shapes=[
            pltpu.VMEM((3, B, B), F32),
            pltpu.VMEM((B, B), F32),
            pltpu.VMEM((8, B), F32),
        ],
        compiler_params=params(),
        cost_estimate=cost(2e10, 12 << 20),
        name="mix_backward",
    )(index, received, received, weights, weights, weights, cots, module, states, fading, gain)


def attention_grads(received, turned, weights, mixed, cots, per=4):
    blocks = received.shape[0]
    steps = blocks // 2 // per
    group = 2 * per

    def kernel(x, turned_ref, w0_ref, w1_ref, w2_ref, m_ref, cot_ref, out, dk, buf, sem):
        grid_step = pl.program_id(0)

        def leaving(b):
            return pltpu.make_async_copy(buf.at[b], out.at[b], sem.at[b])

        @pl.when(grid_step == 0)
        def _():
            dk[...] = jnp.zeros_like(dk)

        for n in range(per):
            step = grid_step * per + n
            window = [jnp.maximum(2 * step - REACH + j, 0) for j in range(REACH + 2)]
            queries = jnp.concatenate([x[2 * n], x[2 * n + 1]], axis=0)
            cot = jnp.concatenate([cot_ref[2 * n], cot_ref[2 * n + 1]], axis=0)
            dp = dot(jnp.concatenate([m_ref[b] for b in window], axis=0), cot, NT)
            w_all = jnp.concatenate([w0_ref[n], w1_ref[n], w2_ref[n]], axis=0)
            columns = []
            for sub in range(2):
                lanes = slice(sub * B, (sub + 1) * B)
                rows = slice(sub * B, sub * B + PAD + B)
                w = w_all[rows, lanes].astype(F32)
                g = dp[rows, lanes]
                ds = (w * (g - jnp.sum(w * g, axis=0, keepdims=True))).astype(BF16)
                zero = jnp.zeros((B, B), BF16)
                columns.append(jnp.concatenate([zero, ds] if sub else [ds, zero], axis=0))
            ds = jnp.concatenate(columns, axis=1)
            dk[pl.ds(pl.multiple_of(step * TWO, TWO), SPAN), :] += dot(ds, queries, NN)
            keys_t = jnp.concatenate([turned_ref[b] for b in window], axis=1)
            dq = (dot(keys_t, ds, NN) * INV_ROOT).T.astype(BF16)
            buf[2 * step, 0:B, :] = dq[0:B]
            buf[2 * step + 1, 0:B, :] = dq[B:]

        def finish(b):
            at = pl.ds(pl.multiple_of(PAD + b * B, B), B)
            buf[b, B:TWO, :] = (dk[at, :] * INV_ROOT).astype(BF16)
            leaving(b).start()

        for j in range(group):
            b = grid_step * group - REACH + j

            @pl.when(b >= 0)
            def _(b=b):
                finish(b)

        @pl.when(grid_step == steps - 1)
        def _():
            for b in range(blocks - REACH, blocks):
                finish(b)
            for b in range(blocks):
                leaving(b).wait()

    everything = lambda a: pl.BlockSpec(a.shape, lambda i: (0, 0, 0))
    return pl.pallas_call(
        kernel,
        grid=(steps,),
        in_specs=[
            pl.BlockSpec((group, B, B), lambda i: (i, QUERIES // B, 0)),
            everything(turned),
            *(
                pl.BlockSpec((per, TWO, TWO), functools.partial(lambda j, i: (i, j, 0), j))
                for j in range(3)
            ),
            everything(mixed),
            pl.BlockSpec((group, B, B), lambda i: (i, 0, 0)),
        ],
        out_specs=pl.BlockSpec(memory_space=pl.ANY),
        out_shape=jax.ShapeDtypeStruct((blocks, TWO, B), BF16),
        scratch_shapes=[
            pltpu.VMEM((PAD + blocks * B, B), F32),
            pltpu.VMEM((blocks, TWO, B), BF16),
            pltpu.SemaphoreType.DMA((blocks,)),
        ],
        compiler_params=params(),
        cost_estimate=cost(2e10, 14 << 20),
        name="attention_grads",
    )(received, turned, weights, weights, weights, mixed, cots)


def exchange(blocks):
    return lax.all_to_all(blocks, "seq", 0, 0, tiled=True)


def local(
    probe_matrix,
    softmax_lookup_matrix,
    acceptance_gate,
    recurrent_lookup_matrix,
    recurrent_payload_matrix,
    upstream_adjoint,
    feature_fading_exponent,
    diagonal_reward_factor,
    spike_fading_exponent,
):
    positions = probe_matrix.shape[1] * lax.axis_size("seq") * lax.axis_size("dp")
    here = lax.axis_index("seq")
    index = here.astype(jnp.int32).reshape(1)
    first_out, cots_out = pack(
        (
            acceptance_gate[0],
            recurrent_lookup_matrix[0],
            recurrent_payload_matrix[0],
            probe_matrix[0],
            softmax_lookup_matrix[0],
        ),
        upstream_adjoint[0],
        spike_fading_exponent[0].T,
    )
    first_out, cots_out, index = lax.optimization_barrier((first_out, cots_out, index))
    first_in = exchange(first_out)
    first_in, cots_out = lax.optimization_barrier((first_in, cots_out))
    cots = exchange(cots_out)
    mixed, module, states, weights, turned = forward(
        first_in, index, feature_fading_exponent, diagonal_reward_factor
    )
    att_back = exchange(attention_grads(first_in, turned, weights, mixed, cots))
    mix_out = mix_backward(
        first_in, weights, cots, module, states, index, feature_fading_exponent, diagonal_reward_factor
    )
    mix_out, att_back = lax.optimization_barrier((mix_out, att_back))
    mix_back = exchange(mix_out)
    dq, dk = unpack(att_back, 2)
    mix_back, dq, dk = lax.optimization_barrier((mix_back, dq, dk))
    parts = mix_back[:, SUMS : SUMS + 6, :].astype(F32)
    sums = jnp.stack(
        [parts[:, 0] + parts[:, 1] + parts[:, 2], parts[:, 3] + parts[:, 4] + parts[:, 5]]
    )
    group = lax.axis_size("dp")
    for bit in range(group.bit_length() - 1):
        sums = sums + lax.ppermute(sums, "dp", [(i, i ^ (1 << bit)) for i in range(group)])
    adjoints = sums * positions ** (-0.5)
    dr, dmk, dmv = unpack(mix_back, 3)
    return (dq[None], dk[None], dr[None], dmk[None], dmv[None], adjoints[0], adjoints[1])


def solution(mesh):
    rows = P("dp", "seq", None)
    return jax.shard_map(
        local,
        mesh=mesh,
        in_specs=(rows,) * 6 + (P(), P(), rows),
        out_specs=(rows,) * 5 + (P(), P()),
        check_vma=False,
    )
```

```python
import functools
import math

import jax
import jax.numpy as jnp
from jax import lax
from jax.experimental import pallas as pl
from jax.experimental.pallas import tpu as pltpu
from jax.sharding import PartitionSpec as P

F32 = jnp.float32
BF16 = jnp.bfloat16
EPSILON = 1e-05
NEG = -1e30
LOG2E = math.log2(math.e)
B = 128
REACH = 4
SPIKE_ROWS = 8
QUERIES = 3 * B
KEYS = 4 * B
SPIKES = 5 * B
SUMS = 3 * B
PAD = REACH * B
TWO = 2 * B
SPAN = PAD + TWO
INV_ROOT = B ** (-0.5)
NN = (((1,), (0,)), ((), ()))
NT = (((1,), (1,)), ((), ()))
TN = (((0,), (0,)), ((), ()))


def dot(a, b, dims):
    return lax.dot_general(a, b, dims, preferred_element_type=F32)


def split(x):
    high = x.astype(BF16)
    return high, (x - high.astype(F32)).astype(BF16)


def dot_a(a, b, dims):
    return dot(a[0], b, dims) + dot(a[1], b, dims)


def dot_b(a, b, dims):
    return dot(a, b[0], dims) + dot(a, b[1], dims)


def dot3(a, b, dims):
    return dot(a[0], b[0], dims) + dot(a[0], b[1], dims) + dot(a[1], b[0], dims)


def iota(axis, shape=(B, B)):
    return lax.broadcasted_iota(jnp.int32, shape, axis)


def vmem():
    return pl.BlockSpec(memory_space=pltpu.VMEM)


def smem():
    return pl.BlockSpec(memory_space=pltpu.SMEM)


def params(mib=58):
    return pltpu.CompilerParams(vmem_limit_bytes=mib << 20)


def cost(flops, nbytes):
    return pl.CostEstimate(flops=int(flops), bytes_accessed=int(nbytes), transcendentals=0)


def three_parts(pair):
    row = iota(0, (SPIKE_ROWS, B))
    tile = jnp.zeros((SPIKE_ROWS, B), F32)
    for n, rest in enumerate(pair):
        for m in range(3):
            part = rest.astype(BF16).astype(F32)
            rest = rest - part
            tile = jnp.where(row == 3 * n + m, part, tile)
    return tile.astype(BF16)


def pack(arrays, cots, spike, per=4):
    heads = cots.shape[1] // B
    count = len(arrays) + 1
    groups = heads // per
    rows = SPIKES + SPIKE_ROWS

    def kernel(*refs):
        sources, surge_ref = refs[:count], refs[count]
        first_out, second, first, held, second_buf, sums, in_sem, out_sem = refs[count + 1 :]

        def entering(a, g):
            columns = slice(g * per * B, (g + 1) * per * B)
            return pltpu.make_async_copy(
                sources[a].at[:, columns], held.at[a, :, columns], in_sem.at[a * groups + g]
            )

        def leaving(g):
            at = slice(g * per, (g + 1) * per)
            return pltpu.make_async_copy(first.at[at], first_out.at[at], out_sem.at[g])

        def leaving_cots(g):
            at = slice(g * per, (g + 1) * per)
            return pltpu.make_async_copy(second_buf.at[at], second.at[at], out_sem.at[groups + g])

        for g in range(groups):
            for a in range(count - 1):
                entering(a, g).start()
        for g in range(groups):
            entering(count - 1, g).start()
        surge = surge_ref[...]
        upto = jnp.where(iota(0) <= iota(1), 1.0, 0.0).astype(F32)
        below = jnp.where(iota(0) < iota(1), 1.0, 0.0).astype(F32)
        for n, mask in enumerate((upto, below)):
            sums[n] = lax.dot_general(
                surge, mask, NN, precision=lax.Precision.HIGHEST, preferred_element_type=F32
            )
        for h in range(heads):
            first[h, SPIKES:, :] = three_parts([sums[n, h : h + 1, :] for n in range(2)])
        for g in range(groups):
            for a in range(count - 1):
                entering(a, g).wait()
                for h in range(g * per, (g + 1) * per):
                    first[h, a * B : (a + 1) * B, :] = held[a, :, h * B : (h + 1) * B]
            leaving(g).start()
        for g in range(groups):
            entering(count - 1, g).wait()
            for h in range(g * per, (g + 1) * per):
                second_buf[h] = held[count - 1, :, h * B : (h + 1) * B]
            leaving_cots(g).start()
        for g in range(groups):
            leaving(g).wait()
            leaving_cots(g).wait()

    hbm = pl.BlockSpec(memory_space=pl.ANY)
    return pl.pallas_call(
        kernel,
        in_specs=[hbm] * count + [vmem()],
        out_specs=[hbm, hbm],
        out_shape=[
            jax.ShapeDtypeStruct((heads, rows, B), BF16),
            jax.ShapeDtypeStruct((heads, B, B), BF16),
        ],
        scratch_shapes=[
            pltpu.VMEM((heads, rows, B), BF16),
            pltpu.VMEM((count, B, heads * B), BF16),
            pltpu.VMEM((heads, B, B), BF16),
            pltpu.VMEM((2, heads, B), F32),
            pltpu.SemaphoreType.DMA((count * groups,)),
            pltpu.SemaphoreType.DMA((2 * groups,)),
        ],
        compiler_params=params(),
        cost_estimate=cost(0, 2 * heads * (rows + B) * B * 2),
        name="pack",
    )(*arrays, cots, spike)


def unpack(packs, counts, per=16):
    heads = packs[0].shape[0]
    total = sum(counts)

    def kernel(*refs):
        outs = iter(refs[len(packs) :])
        for x, count in zip(refs, counts):
            for a in range(count):
                out = next(outs)
                for j in range(per):
                    out[:, j * B : (j + 1) * B] = x[j, a * B : (a + 1) * B, :]

    return pl.pallas_call(
        kernel,
        grid=(heads // per,),
        in_specs=[pl.BlockSpec((per, x.shape[1], B), lambda i: (i, 0, 0)) for x in packs],
        out_specs=[pl.BlockSpec((B, per * B), lambda i: (0, i)) for _ in range(total)],
        out_shape=[jax.ShapeDtypeStruct((B, heads * B), BF16) for _ in range(total)],
        compiler_params=params(20),
        cost_estimate=cost(0, 2 * heads * total * B * B * 2),
        name="unpack",
    )(*packs)


def decay_tables(rate, tables):
    position = iota(0).astype(F32)
    tables[0] = jnp.exp(-position * rate)
    tables[1] = jnp.exp((position + 1.0) * rate)
    tables[2] = jnp.exp(-(B - 1.0 - position) * rate)


def chunk_terms(x, surges, tables, gain, n, exact=True):
    acceptance = x[n, 0:B, :].astype(F32)
    lookup = x[n, B : 2 * B, :].astype(F32)
    payload = x[n, 2 * B : 3 * B, :]
    upto = surges[0:1] + surges[1:2] + surges[2:3]
    below = surges[3:4] + surges[4:5] + surges[5:6]
    diagonal = iota(0) == iota(1)
    below_col = jnp.sum(jnp.where(diagonal, below, 0.0), axis=1, keepdims=True)
    upto_col = jnp.sum(jnp.where(diagonal, upto, 0.0), axis=1, keepdims=True)
    total = upto[:, B - 1 : B]
    lower = iota(1) < iota(0)
    fade = jnp.where(lower, jnp.exp(below_col - upto), 0.0)
    entered = jnp.exp(below_col)
    leaving = jnp.exp(total - upto_col)
    queries = acceptance * tables[0]
    keys = lookup * tables[1]
    keys_end = lookup * tables[2] * leaving
    bonus = jnp.sum(acceptance * gain * lookup, axis=1, keepdims=True)
    if exact:
        queries_s, keys_s = split(queries), split(keys)
        keys_end_s = split(keys_end)
        scores = dot3(queries_s, keys_s, NT)
    else:
        queries_s, keys_s = queries.astype(BF16), keys.astype(BF16)
        keys_end_s = keys_end.astype(BF16)
        scores = dot(queries_s, keys_s, NT)
    scores = scores * fade + jnp.where(diagonal, bonus, 0.0)
    return dict(
        acceptance=acceptance,
        lookup=lookup,
        payload=payload,
        fade=fade,
        entered=entered,
        leaving=leaving,
        total=jnp.exp(total),
        queries=queries,
        queries_s=queries_s,
        keys_s=keys_s,
        keys_end=keys_end,
        keys_end_s=keys_end_s,
        scores=scores,
    )


def head_rows(index, fading, gain):
    return jnp.exp(fading[pl.ds(index, 1), :]), gain[pl.ds(index, 1), :]


def attention_weights(keys, queries, step, weights, n):
    scores_all = dot(keys, queries, NT)
    early = iota(0) > iota(1)
    causal = iota(0) <= iota(1)
    for sub in range(2):
        lanes = slice(sub * B, (sub + 1) * B)
        scores = []
        for j in range(REACH + 1):
            score = scores_all[(sub + j) * B : (sub + j + 1) * B, lanes]
            if j == REACH:
                keep = causal
            else:
                keep = 2 * step + sub + j >= REACH
                if j == 0:
                    keep = early & keep
            scores.append(jnp.where(keep, score, NEG))
        highest = jnp.max(functools.reduce(jnp.maximum, scores), axis=0, keepdims=True)
        raised = [jnp.exp2((score - highest) * (INV_ROOT * LOG2E)) for score in scores]
        share = 1.0 / jnp.sum(sum(raised), axis=0, keepdims=True)
        for j in range(REACH + 1):
            weights[n, (sub + j) * B : (sub + j + 1) * B, lanes] = (raised[j] * share).astype(BF16)
    weights[n, PAD + B :, 0:B] = jnp.zeros((B, B), BF16)
    weights[n, 0:B, B:] = jnp.zeros((B, B), BF16)


def forward(received, index, fading, gain, per=8):
    blocks, rows, _ = received.shape

    def kernel(
        index_ref, x, fading_ref, gain_ref, mixed, module, states, weights, turned,
        tables, memory, kring,
    ):
        rate, gain_row = head_rows(index_ref[0], fading_ref, gain_ref)
        grid_step = pl.program_id(0)

        @pl.when(grid_step == 0)
        def _():
            decay_tables(rate, tables)
            memory[...] = jnp.zeros_like(memory)
            kring[0:PAD, :] = jnp.zeros((PAD, B), BF16)

        whole = jnp.exp(-float(B) * rate)
        state = memory[...]
        for n in range(per):
            keys = x[n, KEYS : KEYS + B, :]
            kring[pl.ds(pl.multiple_of(PAD + (grid_step * per + n) * B, B), B), :] = keys
            turned[n] = keys.T
            c = chunk_terms(
                x, x[n, SPIKES : SPIKES + SPIKE_ROWS, :].astype(F32), tables, gain_row, n
            )
            states[n] = state
            out = dot_a(split(c["scores"]), c["payload"], NN) + c["entered"] * dot3(
                c["queries_s"], split(state), NT
            )
            state = state * (whole * c["total"]) + dot_b(c["payload"], c["keys_end_s"], TN)
            module[n] = out
            average = jnp.mean(out, axis=1, keepdims=True)
            centered = out - average
            variance = jnp.mean(centered * centered, axis=1, keepdims=True)
            mixed[n] = (centered * lax.rsqrt(variance + EPSILON)).astype(BF16)
            if n % 2:
                step = grid_step * (per // 2) + n // 2
                attention_weights(
                    kring[pl.ds(pl.multiple_of(step * TWO, TWO), SPAN), :],
                    jnp.concatenate(
                        [x[n - 1, QUERIES : QUERIES + B, :], x[n, QUERIES : QUERIES + B, :]], axis=0
                    ),
                    step,
                    weights,
                    n // 2,
                )
        memory[...] = state

    block = lambda: pl.BlockSpec((per, B, B), lambda i: (i, 0, 0))
    whole_array = lambda a: pl.BlockSpec(a.shape, lambda i: (0, 0))
    return pl.pallas_call(
        kernel,
        grid=(blocks // per,),
        in_specs=[
            smem(),
            pl.BlockSpec((per, rows, B), lambda i: (i, 0, 0)),
            whole_array(fading),
            whole_array(gain),
        ],
        out_specs=[
            block(),
            block(),
            block(),
            pl.BlockSpec((per // 2, SPAN, TWO), lambda i: (i, 0, 0)),
            block(),
        ],
        out_shape=[
            jax.ShapeDtypeStruct((blocks, B, B), BF16),
            jax.ShapeDtypeStruct((blocks, B, B), F32),
            jax.ShapeDtypeStruct((blocks, B, B), F32),
            jax.ShapeDtypeStruct((blocks // 2, SPAN, TWO), BF16),
            jax.ShapeDtypeStruct((blocks, B, B), BF16),
        ],
        scratch_shapes=[
            pltpu.VMEM((3, B, B), F32),
            pltpu.VMEM((B, B), F32),
            pltpu.VMEM((PAD + blocks * B, B), BF16),
        ],
        compiler_params=params(63),
        cost_estimate=cost(2e10, 18 << 20),
        name="forward",
    )(index, received, fading, gain)


def pair_of(ref, at):
    return jnp.concatenate([ref[2 * at], ref[2 * at + 1]], axis=0)


def mix_backward(received, weights, cots, module, states, index, fading, gain, per=4):
    blocks = received.shape[0]
    rows = SUMS + SPIKE_ROWS
    steps = blocks // per

    def kernel(
        index_ref, x, surge_ref, w0_ref, w1_ref, w2_ref, cot_ref, module_ref, states_ref, fading_ref, gain_ref,
        out, tables, memory, sums,
    ):
        rate, gain_row = head_rows(index_ref[0], fading_ref, gain_ref)

        @pl.when(pl.program_id(0) == 0)
        def _():
            decay_tables(rate, tables)
            memory[...] = jnp.zeros_like(memory)
            sums[...] = jnp.zeros_like(sums)

        whole = jnp.exp(-float(B) * rate)
        position = iota(0).astype(F32)
        distance = jnp.maximum(iota(0) - iota(1) - 1, 0).astype(F32)
        d_state = memory[...]
        d_rate = jnp.zeros((1, B), F32)
        d_gain = jnp.zeros((1, B), F32)
        first = (steps - 1 - pl.program_id(0)) * per
        for n in reversed(range(per)):
            if n % 2:
                pair_at = first // 2 + n // 2
                g_pair = pair_of(cot_ref, pair_at).astype(F32)
                for later in range(3):
                    at = jnp.minimum(pair_at + later, blocks // 2 - 1)
                    seen = pair_of(cot_ref, at)
                    if later:
                        seen = jnp.where(pair_at + later < blocks // 2, seen, jnp.zeros_like(seen))
                    seen_by = (w2_ref, w1_ref, w0_ref)[later]
                    g_pair = g_pair + dot(seen_by[at], seen, NN)
            g = g_pair[B:] if n % 2 else g_pair[0:B]
            c = chunk_terms(x, surge_ref[n].astype(F32), tables, gain_row, n, False)
            value = module_ref[n]
            centered = value - jnp.mean(value, axis=1, keepdims=True)
            variance = jnp.mean(centered * centered, axis=1, keepdims=True)
            scale = lax.rsqrt(variance + EPSILON)
            normed = centered * scale
            grad = scale * (
                g
                - jnp.mean(g, axis=1, keepdims=True)
                - normed * jnp.mean(g * normed, axis=1, keepdims=True)
            )
            grad_2 = split(grad)
            grad_s = grad_2[0]
            state = states_ref[n]
            d_state_s = d_state.astype(BF16)
            payload = c["payload"]
            paired = dot_a(grad_2, payload, NT) * c["fade"]
            paired_s = paired.astype(BF16)
            own = jnp.sum(grad * payload.astype(F32), axis=1, keepdims=True)
            inter = c["entered"] * dot(grad_s, state.astype(BF16), NN)
            d_queries = dot(paired_s, c["keys_s"], NN) + inter
            d_keys = dot(paired_s, c["queries_s"], TN)
            d_end = dot(payload, d_state_s, NN)
            d_payload = dot_b(c["scores"].astype(BF16), grad_2, TN) + dot_b(
                c["keys_end_s"], split(d_state), NT
            )
            out[first + n, 0:B, :] = (
                d_queries * tables[0] + own * gain_row * c["lookup"]
            ).astype(BF16)
            out[first + n, B : 2 * B, :] = (
                d_keys * tables[1]
                + d_end * (tables[2] * c["leaving"])
                + own * gain_row * c["acceptance"]
            ).astype(BF16)
            out[first + n, 2 * B : 3 * B, :] = d_payload.astype(BF16)
            d_gain += jnp.sum(own * c["acceptance"] * c["lookup"], axis=0, keepdims=True)
            spread = dot((paired * distance).astype(BF16), c["keys_s"], NN)
            carried = whole * c["total"]
            d_rate += jnp.sum(
                c["queries"] * (spread + position * inter)
                + (B - 1.0 - position) * c["keys_end"] * d_end
                + (float(B) * carried) * state * d_state,
                axis=0,
                keepdims=True,
            )
            d_state = d_state * carried + dot(
                (grad * c["entered"]).astype(BF16), c["queries_s"], TN
            )
        memory[...] = d_state
        sums[0:1, :] += -rate * d_rate
        sums[1:2, :] += d_gain

        @pl.when(pl.program_id(0) == steps - 1)
        def _():
            tile = three_parts([sums[0:1, :], sums[1:2, :]])
            for b in range(blocks):
                out[b, SUMS:, :] = tile

    back = lambda i: (steps - 1 - i, 0, 0)
    block = lambda: pl.BlockSpec((per, B, B), back)
    whole_array = lambda a: pl.BlockSpec(a.shape, lambda i: (0, 0))
    return pl.pallas_call(
        kernel,
        grid=(steps,),
        in_specs=[
            smem(),
            pl.BlockSpec((per, SUMS, B), back),
            pl.BlockSpec((per, SPIKE_ROWS, B), lambda i: (steps - 1 - i, SPIKES // SPIKE_ROWS, 0)),
            *(
                pl.BlockSpec((blocks // 2, TWO, TWO), functools.partial(lambda j, i: (0, j, 0), j))
                for j in range(3)
            ),
            pl.BlockSpec(cots.shape, lambda i: (0, 0, 0)),
            block(),
            block(),
            whole_array(fading),
            whole_array(gain),
        ],
        out_specs=vmem(),
        out_shape=jax.ShapeDtypeStruct((blocks, rows, B), BF16),
        scratch_shapes=[
            pltpu.VMEM((3, B, B), F32),
            pltpu.VMEM((B, B), F32),
            pltpu.VMEM((8, B), F32),
        ],
        compiler_params=params(),
        cost_estimate=cost(2e10, 12 << 20),
        name="mix_backward",
    )(index, received, received, weights, weights, weights, cots, module, states, fading, gain)


def attention_grads(received, turned, weights, mixed, cots, per=4):
    blocks = received.shape[0]
    steps = blocks // 2 // per
    group = 2 * per

    def kernel(x, turned_ref, w0_ref, w1_ref, w2_ref, m_ref, cot_ref, out, dk, buf, sem):
        grid_step = pl.program_id(0)

        def leaving(b):
            return pltpu.make_async_copy(buf.at[b], out.at[b], sem.at[b])

        @pl.when(grid_step == 0)
        def _():
            dk[...] = jnp.zeros_like(dk)

        def window_of(n):
            first = 2 * (grid_step * per + n) - REACH
            return [jnp.maximum(first + j, 0) for j in range(REACH + 2)]

        def dp_of(n):
            seen = jnp.concatenate([m_ref[b] for b in window_of(n)], axis=0)
            return dot(seen, pair_of(cot_ref, n), NT)

        def ds_of(n, dp):
            w_all = jnp.concatenate([w0_ref[n], w1_ref[n], w2_ref[n]], axis=0)
            columns = []
            for sub in range(2):
                lanes = slice(sub * B, (sub + 1) * B)
                rows = slice(sub * B, sub * B + PAD + B)
                w = w_all[rows, lanes].astype(F32)
                g = dp[rows, lanes]
                ds = (w * (g - jnp.sum(w * g, axis=0, keepdims=True))).astype(BF16)
                zero = jnp.zeros((B, B), BF16)
                columns.append(jnp.concatenate([zero, ds] if sub else [ds, zero], axis=0))
            return jnp.concatenate(columns, axis=1)

        def emit(n, ds):
            step = grid_step * per + n
            dk[pl.ds(pl.multiple_of(step * TWO, TWO), SPAN), :] += dot(ds, pair_of(x, n), NN)
            keys_t = jnp.concatenate([turned_ref[b] for b in window_of(n)], axis=1)
            dq = (dot(keys_t, ds, NN) * INV_ROOT).T.astype(BF16)
            buf[2 * step, 0:B, :] = dq[0:B]
            buf[2 * step + 1, 0:B, :] = dq[B:]

        dp_next, ds_last = dp_of(0), None
        for n in range(per):
            dp = dp_next
            if n + 1 < per:
                dp_next = dp_of(n + 1)
            if ds_last is not None:
                emit(n - 1, ds_last)
            ds_last = ds_of(n, dp)
        emit(per - 1, ds_last)

        def finish(b):
            at = pl.ds(pl.multiple_of(PAD + b * B, B), B)
            buf[b, B:TWO, :] = (dk[at, :] * INV_ROOT).astype(BF16)
            leaving(b).start()

        for j in range(group):
            b = grid_step * group - REACH + j

            @pl.when(b >= 0)
            def _(b=b):
                finish(b)

        @pl.when(grid_step == steps - 1)
        def _():
            for b in range(blocks - REACH, blocks):
                finish(b)
            for b in range(blocks):
                leaving(b).wait()

    everything = lambda a: pl.BlockSpec(a.shape, lambda i: (0, 0, 0))
    return pl.pallas_call(
        kernel,
        grid=(steps,),
        in_specs=[
            pl.BlockSpec((group, B, B), lambda i: (i, QUERIES // B, 0)),
            everything(turned),
            *(
                pl.BlockSpec((per, TWO, TWO), functools.partial(lambda j, i: (i, j, 0), j))
                for j in range(3)
            ),
            everything(mixed),
            pl.BlockSpec((group, B, B), lambda i: (i, 0, 0)),
        ],
        out_specs=pl.BlockSpec(memory_space=pl.ANY),
        out_shape=jax.ShapeDtypeStruct((blocks, TWO, B), BF16),
        scratch_shapes=[
            pltpu.VMEM((PAD + blocks * B, B), F32),
            pltpu.VMEM((blocks, TWO, B), BF16),
            pltpu.SemaphoreType.DMA((blocks,)),
        ],
        compiler_params=params(),
        cost_estimate=cost(2e10, 14 << 20),
        name="attention_grads",
    )(received, turned, weights, weights, weights, mixed, cots)


def exchange(blocks):
    return lax.all_to_all(blocks, "seq", 0, 0, tiled=True)


def local(
    probe_matrix,
    softmax_lookup_matrix,
    acceptance_gate,
    recurrent_lookup_matrix,
    recurrent_payload_matrix,
    upstream_adjoint,
    feature_fading_exponent,
    diagonal_reward_factor,
    spike_fading_exponent,
):
    positions = probe_matrix.shape[1] * lax.axis_size("seq") * lax.axis_size("dp")
    here = lax.axis_index("seq")
    index = here.astype(jnp.int32).reshape(1)
    first_out, cots_out = pack(
        (
            acceptance_gate[0],
            recurrent_lookup_matrix[0],
            recurrent_payload_matrix[0],
            probe_matrix[0],
            softmax_lookup_matrix[0],
        ),
        upstream_adjoint[0],
        spike_fading_exponent[0].T,
    )
    first_out, cots_out, index = lax.optimization_barrier((first_out, cots_out, index))
    first_in = exchange(first_out)
    first_in, cots_out = lax.optimization_barrier((first_in, cots_out))
    cots = exchange(cots_out)
    mixed, module, states, weights, turned = forward(
        first_in, index, feature_fading_exponent, diagonal_reward_factor
    )
    att_back = exchange(attention_grads(first_in, turned, weights, mixed, cots))
    mix_out = mix_backward(
        first_in, weights, cots, module, states, index, feature_fading_exponent, diagonal_reward_factor
    )
    mix_out, att_back = lax.optimization_barrier((mix_out, att_back))
    mix_back = exchange(mix_out)
    mix_back, att_back = lax.optimization_barrier((mix_back, att_back))
    parts = mix_back[:, SUMS : SUMS + 6, :].astype(F32)
    sums = jnp.stack(
        [parts[:, 0] + parts[:, 1] + parts[:, 2], parts[:, 3] + parts[:, 4] + parts[:, 5]]
    )
    group = lax.axis_size("dp")
    for bit in range(group.bit_length() - 1):
        sums = sums + lax.ppermute(sums, "dp", [(i, i ^ (1 << bit)) for i in range(group)])
    adjoints = sums * positions ** (-0.5)
    dq, dk, dr, dmk, dmv = unpack((att_back, mix_back), (2, 3))
    return (dq[None], dk[None], dr[None], dmk[None], dmv[None], adjoints[0], adjoints[1])


def solution(mesh):
    rows = P("dp", "seq", None)
    return jax.shard_map(
        local,
        mesh=mesh,
        in_specs=(rows,) * 6 + (P(), P(), rows),
        out_specs=(rows,) * 5 + (P(), P()),
        check_vma=False,
    )
```

```python
import functools
import math

import jax
import jax.numpy as jnp
from jax import lax
from jax.experimental import pallas as pl
from jax.experimental.pallas import tpu as pltpu
from jax.sharding import PartitionSpec as P

F32 = jnp.float32
BF16 = jnp.bfloat16
EPSILON = 1e-05
NEG = -1e30
LOG2E = math.log2(math.e)
B = 128
REACH = 4
SPIKE_ROWS = 8
QUERIES = 3 * B
KEYS = 4 * B
SPIKES = 5 * B
SUMS = 3 * B
PAD = REACH * B
TWO = 2 * B
SPAN = PAD + TWO
INV_ROOT = B ** (-0.5)
NN = (((1,), (0,)), ((), ()))
NT = (((1,), (1,)), ((), ()))
TN = (((0,), (0,)), ((), ()))


def dot(a, b, dims):
    return lax.dot_general(a, b, dims, preferred_element_type=F32)


def split(x):
    high = x.astype(BF16)
    return high, (x - high.astype(F32)).astype(BF16)


def dot_a(a, b, dims):
    return dot(a[0], b, dims) + dot(a[1], b, dims)


def dot_b(a, b, dims):
    return dot(a, b[0], dims) + dot(a, b[1], dims)


def dot3(a, b, dims):
    return dot(a[0], b[0], dims) + dot(a[0], b[1], dims) + dot(a[1], b[0], dims)


def iota(axis, shape=(B, B)):
    return lax.broadcasted_iota(jnp.int32, shape, axis)


def vmem():
    return pl.BlockSpec(memory_space=pltpu.VMEM)


def smem():
    return pl.BlockSpec(memory_space=pltpu.SMEM)


def params(mib=58):
    return pltpu.CompilerParams(vmem_limit_bytes=mib << 20)


def cost(flops, nbytes):
    return pl.CostEstimate(flops=int(flops), bytes_accessed=int(nbytes), transcendentals=0)


def three_parts(pair):
    row = iota(0, (SPIKE_ROWS, B))
    tile = jnp.zeros((SPIKE_ROWS, B), F32)
    for n, rest in enumerate(pair):
        for m in range(3):
            part = rest.astype(BF16).astype(F32)
            rest = rest - part
            tile = jnp.where(row == 3 * n + m, part, tile)
    return tile.astype(BF16)


def pack(arrays, cots, spike, per=4):
    heads = cots.shape[1] // B
    count = len(arrays) + 1
    groups = heads // per
    rows = SPIKES + SPIKE_ROWS

    def kernel(*refs):
        sources, surge_ref = refs[:count], refs[count]
        first_out, second, first, held, second_buf, sums, in_sem, out_sem = refs[count + 1 :]

        def entering(a, g):
            columns = slice(g * per * B, (g + 1) * per * B)
            return pltpu.make_async_copy(
                sources[a].at[:, columns], held.at[a, :, columns], in_sem.at[a * groups + g]
            )

        def leaving(g):
            at = slice(g * per, (g + 1) * per)
            return pltpu.make_async_copy(first.at[at], first_out.at[at], out_sem.at[g])

        def leaving_cots(g):
            at = slice(g * per, (g + 1) * per)
            return pltpu.make_async_copy(second_buf.at[at], second.at[at], out_sem.at[groups + g])

        for g in range(groups):
            for a in range(count - 1):
                entering(a, g).start()
        for g in range(groups):
            entering(count - 1, g).start()
        surge = surge_ref[...]
        upto = jnp.where(iota(0) <= iota(1), 1.0, 0.0).astype(F32)
        below = jnp.where(iota(0) < iota(1), 1.0, 0.0).astype(F32)
        for n, mask in enumerate((upto, below)):
            sums[n] = lax.dot_general(
                surge, mask, NN, precision=lax.Precision.HIGHEST, preferred_element_type=F32
            )
        for h in range(heads):
            first[h, SPIKES:, :] = three_parts([sums[n, h : h + 1, :] for n in range(2)])
        for g in range(groups):
            for a in range(count - 1):
                entering(a, g).wait()
                for h in range(g * per, (g + 1) * per):
                    first[h, a * B : (a + 1) * B, :] = held[a, :, h * B : (h + 1) * B]
            leaving(g).start()
        for g in range(groups):
            entering(count - 1, g).wait()
            for h in range(g * per, (g + 1) * per):
                second_buf[h] = held[count - 1, :, h * B : (h + 1) * B]
            leaving_cots(g).start()
        for g in range(groups):
            leaving(g).wait()
            leaving_cots(g).wait()

    hbm = pl.BlockSpec(memory_space=pl.ANY)
    return pl.pallas_call(
        kernel,
        in_specs=[hbm] * count + [vmem()],
        out_specs=[hbm, hbm],
        out_shape=[
            jax.ShapeDtypeStruct((heads, rows, B), BF16),
            jax.ShapeDtypeStruct((heads, B, B), BF16),
        ],
        scratch_shapes=[
            pltpu.VMEM((heads, rows, B), BF16),
            pltpu.VMEM((count, B, heads * B), BF16),
            pltpu.VMEM((heads, B, B), BF16),
            pltpu.VMEM((2, heads, B), F32),
            pltpu.SemaphoreType.DMA((count * groups,)),
            pltpu.SemaphoreType.DMA((2 * groups,)),
        ],
        compiler_params=params(),
        cost_estimate=cost(0, 2 * heads * (rows + B) * B * 2),
        name="pack",
    )(*arrays, cots, spike)


def unpack(packs, counts, per=16):
    heads = packs[0].shape[0]
    total = sum(counts)

    def kernel(*refs):
        outs = iter(refs[len(packs) :])
        for x, count in zip(refs, counts):
            for a in range(count):
                out = next(outs)
                for j in range(per):
                    out[:, j * B : (j + 1) * B] = x[j, a * B : (a + 1) * B, :]

    return pl.pallas_call(
        kernel,
        grid=(heads // per,),
        in_specs=[pl.BlockSpec((per, x.shape[1], B), lambda i: (i, 0, 0)) for x in packs],
        out_specs=[pl.BlockSpec((B, per * B), lambda i: (0, i)) for _ in range(total)],
        out_shape=[jax.ShapeDtypeStruct((B, heads * B), BF16) for _ in range(total)],
        compiler_params=params(20),
        cost_estimate=cost(0, 2 * heads * total * B * B * 2),
        name="unpack",
    )(*packs)


def decay_tables(rate, tables):
    position = iota(0).astype(F32)
    tables[0] = jnp.exp(-position * rate)
    tables[1] = jnp.exp((position + 1.0) * rate)
    tables[2] = jnp.exp(-(B - 1.0 - position) * rate)


def chunk_terms(x, surges, tables, gain, n, exact=True):
    acceptance = x[n, 0:B, :].astype(F32)
    lookup = x[n, B : 2 * B, :].astype(F32)
    payload = x[n, 2 * B : 3 * B, :]
    upto = surges[0:1] + surges[1:2] + surges[2:3]
    below = surges[3:4] + surges[4:5] + surges[5:6]
    diagonal = iota(0) == iota(1)
    below_col = jnp.sum(jnp.where(diagonal, below, 0.0), axis=1, keepdims=True)
    upto_col = jnp.sum(jnp.where(diagonal, upto, 0.0), axis=1, keepdims=True)
    total = upto[:, B - 1 : B]
    lower = iota(1) < iota(0)
    fade = jnp.where(lower, jnp.exp(below_col - upto), 0.0)
    entered = jnp.exp(below_col)
    leaving = jnp.exp(total - upto_col)
    queries = acceptance * tables[0]
    keys = lookup * tables[1]
    keys_end = lookup * tables[2] * leaving
    bonus = jnp.sum(acceptance * gain * lookup, axis=1, keepdims=True)
    if exact:
        queries_s, keys_s = split(queries), split(keys)
        keys_end_s = split(keys_end)
        scores = dot3(queries_s, keys_s, NT)
    else:
        queries_s, keys_s = queries.astype(BF16), keys.astype(BF16)
        keys_end_s = keys_end.astype(BF16)
        scores = dot(queries_s, keys_s, NT)
    scores = scores * fade + jnp.where(diagonal, bonus, 0.0)
    return dict(
        acceptance=acceptance,
        lookup=lookup,
        payload=payload,
        fade=fade,
        entered=entered,
        leaving=leaving,
        total=jnp.exp(total),
        queries=queries,
        queries_s=queries_s,
        keys_s=keys_s,
        keys_end=keys_end,
        keys_end_s=keys_end_s,
        scores=scores,
    )


def head_rows(index, fading, gain):
    return jnp.exp(fading[pl.ds(index, 1), :]), gain[pl.ds(index, 1), :]


def attention_weights(keys, queries, step, weights, n):
    scores_all = dot(keys, queries, NT)
    early = iota(0) > iota(1)
    causal = iota(0) <= iota(1)
    for sub in range(2):
        lanes = slice(sub * B, (sub + 1) * B)
        scores = []
        for j in range(REACH + 1):
            score = scores_all[(sub + j) * B : (sub + j + 1) * B, lanes]
            if j == REACH:
                keep = causal
            else:
                keep = 2 * step + sub + j >= REACH
                if j == 0:
                    keep = early & keep
            scores.append(jnp.where(keep, score, NEG))
        highest = jnp.max(functools.reduce(jnp.maximum, scores), axis=0, keepdims=True)
        raised = [jnp.exp2((score - highest) * (INV_ROOT * LOG2E)) for score in scores]
        share = 1.0 / jnp.sum(sum(raised), axis=0, keepdims=True)
        for j in range(REACH + 1):
            weights[n, (sub + j) * B : (sub + j + 1) * B, lanes] = (raised[j] * share).astype(BF16)
    weights[n, PAD + B :, 0:B] = jnp.zeros((B, B), BF16)
    weights[n, 0:B, B:] = jnp.zeros((B, B), BF16)


def forward(received, index, fading, gain, per=8):
    blocks, rows, _ = received.shape

    def kernel(
        index_ref, x, fading_ref, gain_ref, mixed, module, states, weights, turned,
        tables, memory, kring,
    ):
        rate, gain_row = head_rows(index_ref[0], fading_ref, gain_ref)
        grid_step = pl.program_id(0)

        @pl.when(grid_step == 0)
        def _():
            decay_tables(rate, tables)
            memory[...] = jnp.zeros_like(memory)
            kring[0:PAD, :] = jnp.zeros((PAD, B), BF16)

        whole = jnp.exp(-float(B) * rate)
        state = memory[...]
        for n in range(per):
            keys = x[n, KEYS : KEYS + B, :]
            kring[pl.ds(pl.multiple_of(PAD + (grid_step * per + n) * B, B), B), :] = keys
            turned[n] = keys.T
            c = chunk_terms(
                x, x[n, SPIKES : SPIKES + SPIKE_ROWS, :].astype(F32), tables, gain_row, n
            )
            states[n] = state
            out = dot_a(split(c["scores"]), c["payload"], NN) + c["entered"] * dot3(
                c["queries_s"], split(state), NT
            )
            state = state * (whole * c["total"]) + dot_b(c["payload"], c["keys_end_s"], TN)
            module[n] = out
            average = jnp.mean(out, axis=1, keepdims=True)
            centered = out - average
            variance = jnp.mean(centered * centered, axis=1, keepdims=True)
            mixed[n] = (centered * lax.rsqrt(variance + EPSILON)).astype(BF16)
            if n % 2:
                step = grid_step * (per // 2) + n // 2
                attention_weights(
                    kring[pl.ds(pl.multiple_of(step * TWO, TWO), SPAN), :],
                    jnp.concatenate(
                        [x[n - 1, QUERIES : QUERIES + B, :], x[n, QUERIES : QUERIES + B, :]], axis=0
                    ),
                    step,
                    weights,
                    n // 2,
                )
        memory[...] = state

    block = lambda: pl.BlockSpec((per, B, B), lambda i: (i, 0, 0))
    whole_array = lambda a: pl.BlockSpec(a.shape, lambda i: (0, 0))
    return pl.pallas_call(
        kernel,
        grid=(blocks // per,),
        in_specs=[
            smem(),
            pl.BlockSpec((per, rows, B), lambda i: (i, 0, 0)),
            whole_array(fading),
            whole_array(gain),
        ],
        out_specs=[
            block(),
            block(),
            block(),
            pl.BlockSpec((per // 2, SPAN, TWO), lambda i: (i, 0, 0)),
            block(),
        ],
        out_shape=[
            jax.ShapeDtypeStruct((blocks, B, B), BF16),
            jax.ShapeDtypeStruct((blocks, B, B), F32),
            jax.ShapeDtypeStruct((blocks, B, B), F32),
            jax.ShapeDtypeStruct((blocks // 2, SPAN, TWO), BF16),
            jax.ShapeDtypeStruct((blocks, B, B), BF16),
        ],
        scratch_shapes=[
            pltpu.VMEM((3, B, B), F32),
            pltpu.VMEM((B, B), F32),
            pltpu.VMEM((PAD + blocks * B, B), BF16),
        ],
        compiler_params=params(63),
        cost_estimate=cost(2e10, 18 << 20),
        name="forward",
    )(index, received, fading, gain)


def pair_of(ref, at):
    return jnp.concatenate([ref[2 * at], ref[2 * at + 1]], axis=0)


def mix_backward(received, weights, cots, module, states, index, fading, gain, per=4):
    blocks = received.shape[0]
    rows = SUMS + SPIKE_ROWS
    steps = blocks // per

    def kernel(
        index_ref, x, surge_ref, w0_ref, w1_ref, w2_ref, cot_ref, module_ref, states_ref, fading_ref, gain_ref,
        out, tables, memory, sums,
    ):
        rate, gain_row = head_rows(index_ref[0], fading_ref, gain_ref)

        @pl.when(pl.program_id(0) == 0)
        def _():
            decay_tables(rate, tables)
            memory[...] = jnp.zeros_like(memory)
            sums[...] = jnp.zeros_like(sums)

        whole = jnp.exp(-float(B) * rate)
        position = iota(0).astype(F32)
        distance = jnp.maximum(iota(0) - iota(1) - 1, 0).astype(F32)
        d_state = memory[...]
        d_rate = jnp.zeros((1, B), F32)
        d_gain = jnp.zeros((1, B), F32)
        first = (steps - 1 - pl.program_id(0)) * per
        for n in reversed(range(per)):
            if n % 2:
                pair_at = first // 2 + n // 2
                g_pair = pair_of(cot_ref, pair_at).astype(F32)
                for later in range(3):
                    at = jnp.minimum(pair_at + later, blocks // 2 - 1)
                    seen = pair_of(cot_ref, at)
                    if later:
                        seen = jnp.where(pair_at + later < blocks // 2, seen, jnp.zeros_like(seen))
                    seen_by = (w2_ref, w1_ref, w0_ref)[later]
                    g_pair = g_pair + dot(seen_by[at], seen, NN)
            g = g_pair[B:] if n % 2 else g_pair[0:B]
            c = chunk_terms(x, surge_ref[n].astype(F32), tables, gain_row, n, False)
            value = module_ref[n]
            centered = value - jnp.mean(value, axis=1, keepdims=True)
            variance = jnp.mean(centered * centered, axis=1, keepdims=True)
            scale = lax.rsqrt(variance + EPSILON)
            normed = centered * scale
            grad = scale * (
                g
                - jnp.mean(g, axis=1, keepdims=True)
                - normed * jnp.mean(g * normed, axis=1, keepdims=True)
            )
            grad_2 = split(grad)
            grad_s = grad_2[0]
            state = states_ref[n]
            d_state_s = d_state.astype(BF16)
            payload = c["payload"]
            paired = dot_a(grad_2, payload, NT) * c["fade"]
            paired_s = paired.astype(BF16)
            own = jnp.sum(grad * payload.astype(F32), axis=1, keepdims=True)
            inter = c["entered"] * dot(grad_s, state.astype(BF16), NN)
            d_queries = dot(paired_s, c["keys_s"], NN) + inter
            d_keys = dot(paired_s, c["queries_s"], TN)
            d_end = dot(payload, d_state_s, NN)
            d_payload = dot_b(c["scores"].astype(BF16), grad_2, TN) + dot_b(
                c["keys_end_s"], split(d_state), NT
            )
            out[first + n, 0:B, :] = (
                d_queries * tables[0] + own * gain_row * c["lookup"]
            ).astype(BF16)
            out[first + n, B : 2 * B, :] = (
                d_keys * tables[1]
                + d_end * (tables[2] * c["leaving"])
                + own * gain_row * c["acceptance"]
            ).astype(BF16)
            out[first + n, 2 * B : 3 * B, :] = d_payload.astype(BF16)
            d_gain += jnp.sum(own * c["acceptance"] * c["lookup"], axis=0, keepdims=True)
            spread = dot((paired * distance).astype(BF16), c["keys_s"], NN)
            carried = whole * c["total"]
            d_rate += jnp.sum(
                c["queries"] * (spread + position * inter)
                + (B - 1.0 - position) * c["keys_end"] * d_end
                + (float(B) * carried) * state * d_state,
                axis=0,
                keepdims=True,
            )
            d_state = d_state * carried + dot(
                (grad * c["entered"]).astype(BF16), c["queries_s"], TN
            )
        memory[...] = d_state
        sums[0:1, :] += -rate * d_rate
        sums[1:2, :] += d_gain

        @pl.when(pl.program_id(0) == steps - 1)
        def _():
            tile = three_parts([sums[0:1, :], sums[1:2, :]])
            for b in range(blocks):
                out[b, SUMS:, :] = tile

    back = lambda i: (steps - 1 - i, 0, 0)
    block = lambda: pl.BlockSpec((per, B, B), back)
    whole_array = lambda a: pl.BlockSpec(a.shape, lambda i: (0, 0))
    return pl.pallas_call(
        kernel,
        grid=(steps,),
        in_specs=[
            smem(),
            pl.BlockSpec((per, SUMS, B), back),
            pl.BlockSpec((per, SPIKE_ROWS, B), lambda i: (steps - 1 - i, SPIKES // SPIKE_ROWS, 0)),
            *(
                pl.BlockSpec((blocks // 2, TWO, TWO), functools.partial(lambda j, i: (0, j, 0), j))
                for j in range(3)
            ),
            pl.BlockSpec(cots.shape, lambda i: (0, 0, 0)),
            block(),
            block(),
            whole_array(fading),
            whole_array(gain),
        ],
        out_specs=vmem(),
        out_shape=jax.ShapeDtypeStruct((blocks, rows, B), BF16),
        scratch_shapes=[
            pltpu.VMEM((3, B, B), F32),
            pltpu.VMEM((B, B), F32),
            pltpu.VMEM((8, B), F32),
        ],
        compiler_params=params(),
        cost_estimate=cost(2e10, 12 << 20),
        name="mix_backward",
    )(index, received, received, weights, weights, weights, cots, module, states, fading, gain)


def attention_grads(received, turned, weights, mixed, cots, per=4):
    blocks = received.shape[0]
    steps = blocks // 2 // per
    group = 2 * per

    def kernel(x, turned_ref, w0_ref, w1_ref, w2_ref, m_ref, cot_ref, out, dk, buf, sem):
        grid_step = pl.program_id(0)

        def leaving(b):
            return pltpu.make_async_copy(buf.at[b], out.at[b], sem.at[b])

        @pl.when(grid_step == 0)
        def _():
            dk[...] = jnp.zeros_like(dk)

        def window_of(n):
            first = 2 * (grid_step * per + n) - REACH
            return [jnp.maximum(first + j, 0) for j in range(REACH + 2)]

        def dp_of(n):
            seen = jnp.concatenate([m_ref[b] for b in window_of(n)], axis=0)
            return dot(seen, pair_of(cot_ref, n), NT)

        def ds_of(n, dp):
            w_all = jnp.concatenate([w0_ref[n], w1_ref[n], w2_ref[n]], axis=0)
            columns = []
            for sub in range(2):
                lanes = slice(sub * B, (sub + 1) * B)
                rows = slice(sub * B, sub * B + PAD + B)
                w = w_all[rows, lanes].astype(F32)
                g = dp[rows, lanes]
                ds = (w * (g - jnp.sum(w * g, axis=0, keepdims=True))).astype(BF16)
                zero = jnp.zeros((B, B), BF16)
                columns.append(jnp.concatenate([zero, ds] if sub else [ds, zero], axis=0))
            return jnp.concatenate(columns, axis=1)

        def emit(n, ds):
            step = grid_step * per + n
            dk[pl.ds(pl.multiple_of(step * TWO, TWO), SPAN), :] += dot(ds, pair_of(x, n), NN)
            keys_t = jnp.concatenate([turned_ref[b] for b in window_of(n)], axis=1)
            dq = (dot(keys_t, ds, NN) * INV_ROOT).T.astype(BF16)
            buf[2 * step, 0:B, :] = dq[0:B]
            buf[2 * step + 1, 0:B, :] = dq[B:]

        dp_next, ds_last = dp_of(0), None
        for n in range(per):
            dp = dp_next
            if n + 1 < per:
                dp_next = dp_of(n + 1)
            if ds_last is not None:
                emit(n - 1, ds_last)
            ds_last = ds_of(n, dp)
        emit(per - 1, ds_last)

        def finish(b):
            at = pl.ds(pl.multiple_of(PAD + b * B, B), B)
            buf[b, B:TWO, :] = (dk[at, :] * INV_ROOT).astype(BF16)
            leaving(b).start()

        for j in range(group):
            b = grid_step * group - REACH + j

            @pl.when(b >= 0)
            def _(b=b):
                finish(b)

        @pl.when(grid_step == steps - 1)
        def _():
            for b in range(blocks - REACH, blocks):
                finish(b)
            for b in range(blocks):
                leaving(b).wait()

    everything = lambda a: pl.BlockSpec(a.shape, lambda i: (0, 0, 0))
    return pl.pallas_call(
        kernel,
        grid=(steps,),
        in_specs=[
            pl.BlockSpec((group, B, B), lambda i: (i, QUERIES // B, 0)),
            everything(turned),
            *(
                pl.BlockSpec((per, TWO, TWO), functools.partial(lambda j, i: (i, j, 0), j))
                for j in range(3)
            ),
            everything(mixed),
            pl.BlockSpec((group, B, B), lambda i: (i, 0, 0)),
        ],
        out_specs=pl.BlockSpec(memory_space=pl.ANY),
        out_shape=jax.ShapeDtypeStruct((blocks, TWO, B), BF16),
        scratch_shapes=[
            pltpu.VMEM((PAD + blocks * B, B), F32),
            pltpu.VMEM((blocks, TWO, B), BF16),
            pltpu.SemaphoreType.DMA((blocks,)),
        ],
        compiler_params=params(),
        cost_estimate=cost(2e10, 14 << 20),
        name="attention_grads",
    )(received, turned, weights, weights, weights, mixed, cots)


def exchange(blocks):
    return lax.all_to_all(blocks, "seq", 0, 0, tiled=True)


def local(
    probe_matrix,
    softmax_lookup_matrix,
    acceptance_gate,
    recurrent_lookup_matrix,
    recurrent_payload_matrix,
    upstream_adjoint,
    feature_fading_exponent,
    diagonal_reward_factor,
    spike_fading_exponent,
):
    positions = probe_matrix.shape[1] * lax.axis_size("seq") * lax.axis_size("dp")
    here = lax.axis_index("seq")
    index = here.astype(jnp.int32).reshape(1)
    first_out, cots_out = pack(
        (
            acceptance_gate[0],
            recurrent_lookup_matrix[0],
            recurrent_payload_matrix[0],
            probe_matrix[0],
            softmax_lookup_matrix[0],
        ),
        upstream_adjoint[0],
        spike_fading_exponent[0].T,
    )
    first_out, cots_out, index = lax.optimization_barrier((first_out, cots_out, index))
    first_in = exchange(first_out)
    first_in, cots_out = lax.optimization_barrier((first_in, cots_out))
    cots = exchange(cots_out)
    mixed, module, states, weights, turned = forward(
        first_in, index, feature_fading_exponent, diagonal_reward_factor
    )
    att_back = exchange(attention_grads(first_in, turned, weights, mixed, cots))
    mix_out = mix_backward(
        first_in, weights, cots, module, states, index, feature_fading_exponent, diagonal_reward_factor
    )
    mix_out, att_back = lax.optimization_barrier((mix_out, att_back))
    mix_back = exchange(mix_out)
    mix_back, att_back = lax.optimization_barrier((mix_back, att_back))
    parts = mix_back[:, SUMS : SUMS + 6, :].astype(F32)
    sums = jnp.stack(
        [parts[:, 0] + parts[:, 1] + parts[:, 2], parts[:, 3] + parts[:, 4] + parts[:, 5]]
    )
    group = lax.axis_size("dp")
    other = lax.ppermute(sums, "dp", [(i, i ^ 1) for i in range(group)])
    other, (dq, dk) = lax.optimization_barrier((other, unpack((att_back,), (2,))))
    sums = sums + other
    sums = sums + lax.ppermute(sums, "dp", [(i, i ^ 2) for i in range(group)])
    adjoints = sums * positions ** (-0.5)
    dr, dmk, dmv = unpack((mix_back,), (3,))
    return (dq[None], dk[None], dr[None], dmk[None], dmv[None], adjoints[0], adjoints[1])


def solution(mesh):
    rows = P("dp", "seq", None)
    return jax.shard_map(
        local,
        mesh=mesh,
        in_specs=(rows,) * 6 + (P(), P(), rows),
        out_specs=(rows,) * 5 + (P(), P()),
        check_vma=False,
    )
```
